256 devices in a mesh: dp: 32 (over z_lo, x, core), fac: 8 (over z_hi, y).
Axes of the slice: x: 4, y: 4, z: 8 (z_hi: 2, z_lo: 4; z = z_hi * 4 + z_lo), core: 2. Of those that a mesh axis runs over, the one named last changes fastest.
Arguments:
- occupations: int32 [64, 256], P('dp'), may hold values from 0 to 1, as said below
- stream: bfloat16 [16384, 2048], P('dp', 'fac'), may hold values from -6 to 6
- norm_gain: float32 [2048], replicated, may hold values from 0.1 to 1.9
- probs: bfloat16 [64, 16, 256, 256], P('dp', 'fac'), may hold values from 0 to 1, as said below
- w_out: bfloat16 [2048, 2048], P('fac', 'dp'), may hold values from -0.125 to 0.125
- cotangent: bfloat16 [16384, 2048], P('dp', 'fac'), may hold values from -6 to 6
Outputs:
- update: float32 [2048, 2048], P('dp', 'fac')
The draws below stay inside these ranges and needn't reach their ends.
Inputs may be any that keep to these rules, and one draw needn't show every extreme that they name: `occupations`: each sample holds exactly 48 ones. `probs`: within each sample and head, entries with the key after the query are zero and each row sums to one up to bfloat16 rounding.
All inputs are finite; a program needn't handle non-finite values.
Results may differ from the reference program's by a relative error of at most 0.0051.
Values may be sent and summed in bfloat16 or wider, within the bound.
A program may use at most 64 MiB of HBM per device.

```python
import math
import jax
import jax.numpy as jnp
from jax import lax

D = 2048
HEADS = 16
ORBS = 256
NE = 48
ITERS = 2
SAMPLES = 64
TOKENS = 16384


def shuffled(one_key):
    return jax.random.permutation(one_key, ORBS)


def draw_occupations(key, part):
    sample_keys = jax.random.split(jax.random.fold_in(key, 7), SAMPLES)
    orders = jax.vmap(shuffled)(sample_keys)
    return (orders < NE).astype(jnp.int32)


def draw_probs(key, part):
    noise_key = jax.random.fold_in(key, 11)
    rate_key = jax.random.fold_in(key, 12)
    shape = (SAMPLES, HEADS, ORBS, ORBS)
    noise = 1.5 * jax.random.normal(noise_key, shape, jnp.float32)
    rates = jnp.exp(jax.random.uniform(rate_key, (1, HEADS, 1, 1), jnp.float32, math.log(0.5), math.log(8.0))) / ORBS
    query_index = lax.broadcasted_iota(jnp.int32, (ORBS, ORBS), 0)
    key_index = lax.broadcasted_iota(jnp.int32, (ORBS, ORBS), 1)
    distance = (query_index - key_index).astype(jnp.float32)
    scores = noise - rates * distance
    scores = jnp.where(key_index <= query_index, scores, -1e+30)
    scores = scores - jnp.max(scores, axis=-1, keepdims=True)
    weights = jnp.exp(scores)
    return (weights / jnp.sum(weights, axis=-1, keepdims=True)).astype(jnp.bfloat16)


def block_levels(stream_key, extent, pieces, low, largest):
    factor_of, own = 1.0, jax.random.fold_in(stream_key, 6)
    for dim, parts in pieces:
        heights = jnp.exp(jax.random.uniform(jax.random.fold_in(own, dim), (parts,), jnp.float32, low / len(pieces), largest / len(pieces)))
        factor_of = factor_of * jnp.repeat(heights, extent[dim] // parts).reshape([-1 if axis == dim else 1 for axis in range(len(extent))])
    return factor_of


def gaussian(own_key, shape, spread, limit, cuts=(), held_as=jnp.bfloat16):
    gain = block_levels(own_key, shape, cuts, -0.22, 0.18) if cuts else 1.0
    values = jax.random.normal(own_key, shape, jnp.float32) * spread * gain
    return jnp.minimum(jnp.maximum(values, -limit), limit).astype(held_as)


def setup_inputs(seed: int = 0) -> dict:
    seeds = jax.random.split(jax.random.key(seed), 7)
    occupations = draw_occupations(jax.random.fold_in(seeds[6], 71), 0)
    stream = gaussian(seeds[1], (TOKENS, D), 1.0, 6.0, ((0, 32), (1, 8)))
    norm_gain = jnp.clip(1.0 + 0.18 * jax.random.normal(seeds[2], (D,), jnp.float32), 0.1, 1.9)
    probs = draw_probs(jax.random.fold_in(seeds[6], 71), 0)
    w_out = gaussian(seeds[4], (D, D), D ** -0.5, 0.125, ((0, 8), (1, 32)))
    cotangent = gaussian(seeds[5], (TOKENS, D), 1.0, 6.0, ((0, 32), (1, 8)))
    return {"occupations": occupations, "stream": stream, "norm_gain": norm_gain, "probs": probs, "w_out": w_out, "cotangent": cotangent}


damping = 0.1
epsilon = 1e-06
highest = lax.Precision.HIGHEST

def keep_mask(occupations):
    occupied = occupations.astype(jnp.int32)
    before = jnp.cumsum(occupied, axis=1).astype(jnp.int32) - occupied
    position = lax.broadcasted_iota(jnp.int32, occupied.shape, 1)
    forced = (before == NE) | (position - before == ORBS - NE)
    return 1 - forced.astype(jnp.int32)

def newton_schulz(factor):
    identity = jnp.eye(factor.shape[0], dtype=jnp.float32)
    alpha = 1.0 / jnp.sqrt(jnp.sum(factor * factor))
    iterate = 2.0 * alpha * identity - alpha * alpha * factor
    for iteration in range(ITERS - 1):
        product = jnp.dot(factor, iterate, precision=highest)
        iterate = 2.0 * iterate - jnp.dot(iterate, product, precision=highest)
    return iterate

def one_sample(inputs):
    weights, grads = inputs
    return jnp.einsum('hij,ihe->jhe', weights.astype(jnp.float32), grads.astype(jnp.float32))

def reference(occupations, stream, norm_gain, probs, w_out, cotangent):
    values = stream.astype(jnp.float32)
    mean_square = lax.optimization_barrier(jnp.mean(values * values, axis=1, keepdims=True))
    normed = (values * lax.rsqrt(mean_square + epsilon) * norm_gain).astype(jnp.bfloat16)
    keep = keep_mask(occupations).reshape(TOKENS, 1).astype(jnp.bfloat16)
    upstream = cotangent * keep
    out_grad = jnp.dot(upstream, w_out.T, preferred_element_type=jnp.float32).astype(jnp.bfloat16)
    per_head = out_grad.reshape(SAMPLES, ORBS, HEADS, D // HEADS)
    value_grad = lax.map(one_sample, (probs, per_head)).reshape(TOKENS, D).astype(jnp.bfloat16)
    scale = 1.0 / TOKENS
    identity = jnp.eye(D, dtype=jnp.float32)
    a_fac = jnp.dot(normed.T, normed, preferred_element_type=jnp.float32) * scale + damping * identity
    g_fac = jnp.dot(value_grad.T, value_grad, preferred_element_type=jnp.float32) * scale + damping * identity
    grad = jnp.dot(normed.T, value_grad, preferred_element_type=jnp.float32) * scale
    inv_a = newton_schulz(a_fac)
    inv_g = newton_schulz(g_fac)
    pre = jnp.dot(jnp.dot(inv_a, grad, precision=highest), inv_g, precision=highest)
    inner_sum = jnp.sum(grad * pre)
    return pre * (D / jnp.sqrt(inner_sum + epsilon))
```

```python
import jax
import jax.numpy as jnp
from jax import lax
from jax.experimental import pallas as pl
from jax.experimental.pallas import tpu as pltpu
from jax.sharding import PartitionSpec as P

ORBS = 256
NE = 48
TOK = 512
D = 2048
B = 256
R = 64
SCALE = 1.0 / 16384
damping = 0.1
epsilon = 1e-06
bf16 = jnp.bfloat16
f32 = jnp.float32
NSEM = 200


def dot(a, b):
    return lax.dot_general(a, b, (((1,), (0,)), ((), ())), preferred_element_type=f32)


def dot_t(a, b):
    return lax.dot_general(a, b, (((0,), (0,)), ((), ())), preferred_element_type=f32)


def kernel(occ, stream, gain, probs, w_out, cot, out,
           cot_all, st_all, n_all, v_all, w_all, acc, keep_s,
           part, rc_b, s1_b, rx_b, s2_b, rz_b, rzg_b, slab,
           grad_s, tsrc, tdst, tt, xg, xs, nrm_src, nrm, fin, ssem, rsem):
    d = lax.axis_index("dp")
    f = lax.axis_index("fac")
    z, x, c = d // 8, (d // 2) % 4, d % 2
    h, y = f // 4, f % 4

    def at(dh=0, dy=0, dz=0, dx=0, dc=0):
        nd = (((z + dz) % 4) * 4 + (x + dx) % 4) * 2 + (c + dc) % 2
        nf = ((h + dh) % 2) * 4 + (y + dy) % 4
        return {"dp": nd, "fac": nf}

    count = [0]
    started = []

    def copy(src, dst, dev):
        i = count[0]
        count[0] += 1
        return pltpu.make_async_remote_copy(
            src_ref=src, dst_ref=dst, send_sem=ssem.at[i], recv_sem=rsem.at[i],
            device_id=dev, device_id_type=pl.DeviceIdType.MESH)

    def start(cp):
        cp.start()
        started.append(cp)
        return cp

    fac_offs = [(a, b) for a in range(2) for b in range(4) if (a, b) != (0, 0)]
    dp_offs = [(a, b) for a in range(4) for b in range(4) if (a, b) != (0, 0)]

    bar = pltpu.get_barrier_semaphore()

    def greet(dev):
        pl.semaphore_signal(bar, inc=1, device_id=dev, device_id_type=pl.DeviceIdType.MESH)

    for a, b in fac_offs:
        greet(at(dh=a, dy=b))
    for a, b in dp_offs:
        greet(at(dz=a, dx=b))
    greet(at(dc=1))
    own = (d // 4) == f
    for m in range(4):
        @pl.when(jnp.logical_not(own & (d % 4 == m)))
        def _(m=m):
            greet({"dp": 4 * f + m, "fac": d // 4})
    pl.semaphore_wait(bar, 7 + 15 + 1 + 4 - own.astype(jnp.int32))

    class Gather:
        def __init__(self, src, buf):
            self.buf = buf
            self.first = [copy(src.at[pl.ds(k * 256, 256)], buf.at[f, pl.ds(k * 256, 256)], at(dh=1)) for k in range(2)]
            self.ring = [copy(src, buf.at[f], at(dy=j)) for j in (1, 3, 2)]
            other = (1 - h) * 4 + y
            self.fwd = [[copy(buf.at[other, pl.ds(k * 256, 256)], buf.at[other, pl.ds(k * 256, 256)], at(dy=j))
                         for j in (1, 3, 2)] for k in range(2)]

        def begin(self):
            for cp in self.first + self.ring:
                start(cp)

        def middle(self):
            for k in range(2):
                self.first[k].wait_recv()
                for cp in self.fwd[k]:
                    start(cp)

        def finish(self):
            for cp in self.ring + self.fwd[0] + self.fwd[1]:
                cp.wait_recv()

    g_cot = Gather(cot, cot_all)
    g_cot.begin()
    ii = lax.broadcasted_iota(jnp.int32, (R, R), 0)
    jj = lax.broadcasted_iota(jnp.int32, (R, R), 1)
    eye = (ii == jj).astype(bf16)
    w_all[z * 4 + x, c] = lax.dot_general(
        eye, w_out[...], (((1,), (1,)), ((), ())), preferred_element_type=f32).astype(bf16)
    w_me = w_all.at[z * 4 + x, c]
    w_cps = [start(copy(w_me, w_me, at(dz=a, dx=b))) for a, b in dp_offs]

    cot_all[f] = cot[...]
    row = lax.broadcasted_iota(jnp.int32, (ORBS, ORBS), 0)
    col = lax.broadcasted_iota(jnp.int32, (ORBS, ORBS), 1)
    pos = lax.broadcasted_iota(jnp.int32, (ORBS, 1), 0).astype(f32)
    for s in range(2):
        ones = occ[pl.ds(s, 1), :].astype(f32)
        before = jnp.sum(jnp.where(col < row, ones, 0.0), axis=1, keepdims=True)
        forced = (before == float(NE)) | (pos - before == float(ORBS - NE))
        keep_s[pl.ds(s * ORBS, ORBS), :] = jnp.where(forced, 0.0, 1.0)

    g_cot.middle()
    for cp in w_cps:
        cp.wait_recv()
    w_core = start(copy(w_all.at[:, c], w_all.at[:, c], at(dc=1)))
    g_st = Gather(stream, st_all)
    g_cot.finish()
    g_st.begin()
    st_all[f] = stream[...]
    w_core.wait_recv()

    acc[...] = jnp.zeros_like(acc)

    def og(b, _):
        w_blk = w_all[pl.ds(b * 2, 2)].reshape(B, B)
        acc[...] += dot(cot_all[b], w_blk)
        return 0

    lax.fori_loop(0, 8, og, 0)
    for s in range(2):
        rows = pl.ds(s * ORBS, ORBS)
        og_s = (acc[rows, :] * keep_s[rows, :]).astype(bf16)
        for hd in range(2):
            v = dot_t(probs[s, hd], og_s[:, hd * 128:(hd + 1) * 128])
            v_all[f, rows, pl.ds(hd * 128, 128)] = v.astype(bf16)
    g_v = Gather(v_all.at[f], v_all)
    g_v.begin()

    g_st.middle()
    g_v.middle()
    g_st.finish()

    def norm(t, _):
        rows = pl.ds(pl.multiple_of(t * 32, 32), 32)
        sq = jnp.zeros((32, B), f32)
        for b in range(8):
            v = st_all[b, rows, :].astype(f32)
            sq = sq + v * v
        inv = lax.rsqrt(jnp.sum(sq, axis=1, keepdims=True) * (1.0 / D) + epsilon)
        for b in range(8):
            v = st_all[b, rows, :].astype(f32)
            n_all[b, rows, :] = (v * inv * gain[:, b * B:(b + 1) * B]).astype(bf16)
        return 0

    lax.fori_loop(0, TOK // 32, norm, 0)

    def gram(k, left, right):
        def body(b, _):
            p = dot_t(left[b], right[f]) * SCALE
            part[k, pl.ds(b * 2, 2)] = p.astype(bf16).reshape(2, 2, R, B)
            return 0
        lax.fori_loop(0, 8, body, 0)

    core_cp = [copy(part.at[k, :, 1 - c], rc_b.at[k], at(dc=1)) for k in range(3)]
    x_cp = [[copy(s1_b.at[k, :, (x + j) % 4], rx_b.at[k, j - 1], at(dx=j)) for j in (1, 3, 2)] for k in range(3)]

    def core_done(k):
        core_cp[k].wait_recv()

        def body(q, _):
            s1_b[k, q] = (part[k, pl.ds(q * 4, 4), c].astype(f32)
                          + rc_b[k, pl.ds(q * 4, 4)].astype(f32)).astype(bf16)
            return 0
        lax.fori_loop(0, 4, body, 0)
        for cp in x_cp[k]:
            start(cp)

    z_cp = [[copy(s2_b.at[0, (z + j) % 4], rzg_b.at[j - 1], at(dz=j)) for j in (1, 3, 2)]]
    z_cp += [[copy(s2_b.at[k], rz_b.at[k - 1, j - 1], at(dz=j)) for j in (1, 3, 2)] for k in (1, 2)]

    def x_done(k):
        for cp in x_cp[k]:
            cp.wait_recv()
        t = s1_b[k, :, x].astype(f32)
        for j in range(3):
            t = t + rx_b[k, j].astype(f32)
        s2_b[k] = t.astype(bf16)
        for cp in z_cp[k]:
            start(cp)

    agx_cp = [[copy(slab.at[k, :, x, c], slab.at[k, :, x, c], at(dx=j)) for j in (1, 3, 2)] for k in range(2)]
    agc_cp = [copy(slab.at[k, :, :, c], slab.at[k, :, :, c], at(dc=1)) for k in range(2)]

    def z_done(k):
        for cp in z_cp[k]:
            cp.wait_recv()
        if k == 0:
            t = s2_b[0, z].astype(f32)
            for j in range(3):
                t = t + rzg_b[j].astype(f32)
            grad_s[...] = t
            return
        t = s2_b[k].astype(f32)
        for j in range(3):
            t = t + rz_b[k - 1, j].astype(f32)
        slab[k - 1, :, x, c] = t.astype(bf16)
        for cp in agx_cp[k - 1]:
            start(cp)

    def agx_done(k):
        for cp in agx_cp[k - 1]:
            cp.wait_recv()
        start(agc_cp[k - 1])

    nrm_cp = [[copy(nrm_src.at[k], nrm.at[k, f], at(dh=a, dy=b)) for a, b in fac_offs] for k in range(2)]

    def agc_done(k):
        agc_cp[k - 1].wait_recv()

        def body(b, t):
            blk = slab[k - 1, b // 2, pl.ds((b % 2) * 2, 2)].reshape(B, B).astype(f32)
            add = jnp.where((row == col) & (b == f), damping, 0.0)
            blk = blk + add
            return t + jnp.sum(blk * blk, axis=0, keepdims=True)
        t = lax.fori_loop(0, 8, body, jnp.zeros((1, B), f32))
        total = jnp.sum(t, axis=1, keepdims=True)
        nrm_src[k - 1] = jnp.broadcast_to(total, (8, 128))
        nrm[k - 1, f] = jnp.broadcast_to(total, (8, 128))
        for cp in nrm_cp[k - 1]:
            start(cp)

    def alpha_of(k):
        for cp in nrm_cp[k - 1]:
            cp.wait_recv()
        t = nrm[k - 1, 0]
        for b in range(1, 8):
            t = t + nrm[k - 1, b]
        return (1.0 / jnp.sqrt(t))[0:1, 0:1]

    x_own = [None] * 6
    step_cp = [[copy(xs.at[i], xg.at[i, f], at(dh=a, dy=b)) for a, b in fac_offs] for i in range(6)]

    def step_send(i, value):
        v = value.astype(bf16)
        xs[i] = v
        xg[i, f] = v
        x_own[i] = value
        for cp in step_cp[i]:
            start(cp)

    def step_mul(i, k):
        for cp in step_cp[i]:
            cp.wait_recv()
        t = x_own[i] * damping
        for b in range(8):
            t = t + dot(xg[i, b], slab[k - 1, b // 2, (b % 2) * 2:(b % 2) * 2 + 2].reshape(B, B))
        return t

    t_base = []
    for _ in range(2):
        t_base.append(count[0])
        count[0] += 4
    peers = {"fac": d // 4}

    def t_copy(i, m, slot):
        return pltpu.make_async_remote_copy(
            src_ref=tsrc.at[i, m // 2], dst_ref=tdst.at[i, slot], send_sem=ssem.at[t_base[i] + m],
            recv_sem=rsem.at[t_base[i] + slot], device_id={"dp": 4 * f + m, "fac": d // 4},
            device_id_type=pl.DeviceIdType.MESH)

    def t_send(i, value):
        tsrc[i, 0] = value[:, :128]
        tsrc[i, 1] = value[:, 128:]
        slot = d % 4
        for m in range(4):
            here = own & (d % 4 == m)

            @pl.when(here)
            def _(m=m):
                pltpu.make_async_copy(tsrc.at[i, m // 2], tdst.at[i, slot], rsem.at[t_base[i] + slot]).start()

            @pl.when(jnp.logical_not(here))
            def _(m=m):
                t_copy(i, m, slot).start()

    def t_recv(i):
        for k in range(4):
            t_copy(i, k, k).wait_recv()
        s = jnp.concatenate([tdst[i, k] for k in range(4)], axis=0)
        tt[...] = s.T
        return tt[pl.ds(pl.multiple_of((d % 2) * R, R), R), :]

    gram(0, n_all, v_all)
    start(core_cp[0])
    gram(1, n_all, n_all)
    start(core_cp[1])
    core_done(0)
    core_done(1)
    g_v.finish()
    gram(2, v_all, v_all)
    start(core_cp[2])
    x_done(0)
    x_done(1)
    core_done(2)
    z_done(0)
    t_send(0, grad_s[...])
    z_done(1)
    x_done(2)
    agx_done(1)
    x0 = t_recv(0)
    agc_done(1)
    step_send(0, x0)
    z_done(2)
    a_alpha = alpha_of(1)
    c1 = 4.0 * x0 - a_alpha * step_mul(0, 1)
    step_send(1, c1)
    agx_done(2)
    c2 = 6.0 * x0 - a_alpha * step_mul(1, 1)
    step_send(2, c2)
    agc_done(2)
    c3 = 4.0 * x0 - a_alpha * step_mul(2, 1)
    t_send(1, c3)
    g_alpha = alpha_of(2)
    l0 = t_recv(1)
    step_send(3, l0)
    c1 = 4.0 * l0 - g_alpha * step_mul(3, 2)
    step_send(4, c1)
    c2 = 6.0 * l0 - g_alpha * step_mul(4, 2)
    step_send(5, c2)
    c3 = 4.0 * l0 - g_alpha * step_mul(5, 2)
    pre = c3 * (a_alpha * g_alpha)

    part_sum = jnp.sum(jnp.sum(grad_s[...] * pre, axis=0, keepdims=True), axis=1, keepdims=True)
    fin[0] = jnp.broadcast_to(part_sum, (8, 128))
    cp = start(copy(fin.at[0], fin.at[1], at(dc=1)))
    cp.wait_recv()
    fin[2] = fin[0] + fin[1]
    cps = [start(copy(fin.at[2], fin.at[3 + i], at(dz=a, dx=b))) for i, (a, b) in enumerate(dp_offs)]
    for cp in cps:
        cp.wait_recv()
    t = fin[2]
    for i in range(15):
        t = t + fin[3 + i]
    fin[18] = t
    cps = [start(copy(fin.at[18], fin.at[19 + i], at(dh=a, dy=b))) for i, (a, b) in enumerate(fac_offs)]
    for cp in cps:
        cp.wait_recv()
    for i in range(7):
        t = t + fin[19 + i]
    inner = t[0:1, 0:1]
    out[...] = pre * (float(D) / jnp.sqrt(inner + epsilon))

    for cp in started:
        cp.wait_send()
    for i in range(2):
        for m in range(4):
            @pl.when(jnp.logical_not(own & (d % 4 == m)))
            def _(i=i, m=m):
                t_copy(i, m, 0).wait_send()
    assert count[0] <= NSEM


def per_device(occupations, stream, norm_gain, probs, w_out, cotangent):
    vm = pl.BlockSpec(memory_space=pltpu.VMEM)
    V = pltpu.VMEM
    return pl.pallas_call(
        kernel,
        out_shape=jax.ShapeDtypeStruct((R, B), f32),
        in_specs=[vm] * 6,
        out_specs=vm,
        scratch_shapes=[
            V((8, TOK, B), bf16),
            V((8, TOK, B), bf16),
            V((8, TOK, B), bf16),
            V((8, TOK, B), bf16),
            V((16, 2, R, B), bf16),
            V((TOK, B), f32),
            V((TOK, 1), f32),
            V((3, 16, 2, R, B), bf16),
            V((3, 16, R, B), bf16),
            V((3, 4, 4, R, B), bf16),
            V((3, 3, 4, R, B), bf16),
            V((3, 4, R, B), bf16),
            V((2, 3, 4, R, B), bf16),
            V((3, R, B), bf16),
            V((2, 4, 4, 2, R, B), bf16),
            V((R, B), f32),
            V((2, 2, R, 128), f32),
            V((2, 4, R, 128), f32),
            V((128, B), f32),
            V((6, 8, R, B), bf16),
            V((6, R, B), bf16),
            V((2, 8, 128), f32),
            V((2, 8, 8, 128), f32),
            V((26, 8, 128), f32),
            pltpu.SemaphoreType.DMA((NSEM,)),
            pltpu.SemaphoreType.DMA((NSEM,)),
        ],
        compiler_params=pltpu.CompilerParams(
            collective_id=0, has_side_effects=True, vmem_limit_bytes=56 << 20),
    )(occupations, stream, norm_gain.reshape(1, D), probs, w_out, cotangent)


def solution(mesh):
    placed = (
        P("dp", None),
        P("dp", "fac"),
        P(),
        P("dp", "fac", None, None),
        P("fac", "dp"),
        P("dp", "fac"),
    )
    return jax.shard_map(
        per_device, mesh=mesh, in_specs=placed, out_specs=P("dp", "fac"), check_vma=False
    )
```

```python
import jax
import jax.numpy as jnp
from jax import lax
from jax.experimental import pallas as pl
from jax.experimental.pallas import tpu as pltpu
from jax.sharding import PartitionSpec as P

ORBS = 256
NE = 48
TOK = 512
D = 2048
B = 256
R = 64
SCALE = 1.0 / 16384
damping = 0.1
epsilon = 1e-06
bf16 = jnp.bfloat16
f32 = jnp.float32
NSEM = 240


def dot(a, b):
    return lax.dot_general(a, b, (((1,), (0,)), ((), ())), preferred_element_type=f32)


def dot_t(a, b):
    return lax.dot_general(a, b, (((0,), (0,)), ((), ())), preferred_element_type=f32)


def kernel(occ, stream_h, gain, probs_h, w_h, cot_h, out,
           cot_all, st_all, n_all, v_all, w_all, probs, acc, keep_s,
           part, rc_b, s1_b, rx_b, s2_b, rz_b, slab,
           grad2, gx, tsrc, tdst, tt, xg, nsrc, nbuf, fin, lsem, ssem, rsem):
    d = lax.axis_index("dp")
    f = lax.axis_index("fac")
    z, x, c = d // 8, (d // 2) % 4, d % 2
    h, y = f // 4, f % 4
    fd = d // 4
    mesh_id = pl.DeviceIdType.MESH

    def at(dh=0, dy=0, dz=0, dx=0, dc=0):
        nd = (((z + dz) % 4) * 4 + (x + dx) % 4) * 2 + (c + dc) % 2
        nf = ((h + dh) % 2) * 4 + (y + dy) % 4
        return {"dp": nd, "fac": nf}

    count = [0]
    started = []

    def copy(src, dst, dev):
        i = count[0]
        count[0] += 1
        return pltpu.make_async_remote_copy(
            src_ref=src, dst_ref=dst, send_sem=ssem.at[i], recv_sem=rsem.at[i],
            device_id=dev, device_id_type=pl.DeviceIdType.MESH)

    def start(cp):
        cp.start()
        started.append(cp)
        return cp

    fac_offs = [(1, 2), (1, 1), (1, 3), (1, 0), (0, 2), (0, 1), (0, 3)]
    dp_offs = [(a, b) for a in range(4) for b in range(4) if (a, b) != (0, 0)]
    z8_offs = [(1, 0), (1, 1), (1, 2), (1, 3), (0, 2), (0, 1), (0, 3)]

    bar = pltpu.get_barrier_semaphore()

    def greet(dev):
        pl.semaphore_signal(bar, inc=1, device_id=dev, device_id_type=mesh_id)

    for a, b in fac_offs:
        greet(at(dh=a, dy=b))
    for a, b in dp_offs:
        greet(at(dz=a, dx=b))
    greet(at(dc=1))
    for j in (1, 2, 3):
        greet(at(dh=1, dz=j))
    own0 = fd == f
    own1 = fd % 4 == y
    for e in range(2):
        for m in range(4):
            me = d == 4 * (e * 4 + y) + m

            @pl.when(jnp.logical_not(own0 & me))
            def _(e=e, m=m):
                greet({"dp": 4 * (e * 4 + y) + m, "fac": fd})

            @pl.when(jnp.logical_not(own1 & me))
            def _(e=e, m=m):
                greet({"dp": 4 * (e * 4 + y) + m, "fac": h * 4 + fd % 4})

    local = [pltpu.make_async_copy(a, b, lsem.at[i]) for i, (a, b) in enumerate([
        (stream_h, st_all.at[f]), (cot_h, cot_all.at[f]), (w_h, w_all.at[z * 4 + x, c]), (probs_h, probs)])]
    for cp in local:
        cp.start()
    pl.semaphore_wait(bar, 7 + 15 + 1 + 3 + 16 - own0.astype(jnp.int32) - own1.astype(jnp.int32))

    class Gather:
        def __init__(self, buf):
            other = (1 - h) * 4 + y
            rows = [pl.ds(k * 256, 256) for k in range(2)]
            self.first = [copy(buf.at[f, r], buf.at[f, r], at(dh=1)) for r in rows]
            self.ring = [copy(buf.at[f], buf.at[f], at(dy=j)) for j in (1, 3, 2)]
            self.fwd = [[copy(buf.at[other, r], buf.at[other, r], at(dy=j)) for j in (1, 3, 2)] for r in rows]

        def begin_z(self):
            for cp in self.first:
                start(cp)

        def begin_y(self):
            for cp in self.ring:
                start(cp)

        def middle(self):
            for k in range(2):
                self.first[k].wait_recv()
                for cp in self.fwd[k]:
                    start(cp)

        def finish_a(self):
            for cp in self.ring + self.fwd[0]:
                cp.wait_recv()

        def finish_b(self):
            for cp in self.fwd[1]:
                cp.wait_recv()

    g_st, g_cot, g_v = Gather(st_all), Gather(cot_all), Gather(v_all)
    local[0].wait()
    g_st.begin_z()
    g_st.begin_y()
    row = lax.broadcasted_iota(jnp.int32, (ORBS, ORBS), 0)
    col = lax.broadcasted_iota(jnp.int32, (ORBS, ORBS), 1)
    pos = lax.broadcasted_iota(jnp.int32, (ORBS, 1), 0).astype(f32)
    for s in range(2):
        ones = occ[pl.ds(s, 1), :].astype(f32)
        before = jnp.sum(jnp.where(col < row, ones, 0.0), axis=1, keepdims=True)
        forced = (before == float(NE)) | (pos - before == float(ORBS - NE))
        keep_s[pl.ds(s * ORBS, ORBS), :] = jnp.where(forced, 0.0, 1.0)
    for cp in local[1:]:
        cp.wait()
    g_st.middle()
    g_cot.begin_z()
    w_me = w_all.at[z * 4 + x, c]
    w_cps = [start(copy(w_me, w_me, at(dz=a, dx=b))) for a, b in dp_offs]
    w_core = copy(w_all.at[:, c], w_all.at[:, c], at(dc=1))
    g_st.finish_a()
    g_cot.begin_y()
    g_st.finish_b()

    def norm(t, _):
        rows = pl.ds(pl.multiple_of(t * 32, 32), 32)
        sq = jnp.zeros((32, B), f32)
        for b in range(8):
            v = st_all[b, rows, :].astype(f32)
            sq = sq + v * v
        inv = lax.rsqrt(jnp.sum(sq, axis=1, keepdims=True) * (1.0 / D) + epsilon)
        for b in range(8):
            v = st_all[b, rows, :].astype(f32)
            n_all[b, rows, :] = (v * inv * gain[:, b * B:(b + 1) * B]).astype(bf16)
        return 0

    def gram(k, left, right):
        def body(b, _):
            p = dot_t(left[b], right[f]) * SCALE
            part[k, pl.ds(b * 2, 2)] = p.astype(bf16).reshape(2, 2, R, B)
            return 0
        lax.fori_loop(0, 8, body, 0)

    core_cp = [copy(part.at[k, :, 1 - c], rc_b.at[k], at(dc=1)) for k in range(3)]
    x_cp = [[copy(s1_b.at[k, :, (x + j) % 4], rx_b.at[k, j - 1], at(dx=j)) for j in (1, 3, 2)] for k in range(3)]

    def core_done(k):
        core_cp[k].wait_recv()

        def body(q, _):
            s1_b[k, q] = (part[k, pl.ds(q * 4, 4), c].astype(f32)
                          + rc_b[k, pl.ds(q * 4, 4)].astype(f32)).astype(bf16)
            return 0
        lax.fori_loop(0, 4, body, 0)
        for cp in x_cp[k]:
            start(cp)

    z_cp = [[copy(s2_b.at[k, (z + j) % 4], rz_b.at[k, j - 1], at(dz=j)) for j in (2, 1, 3)] for k in range(3)]

    def x_done(k):
        for cp in x_cp[k]:
            cp.wait_recv()
        t = s1_b[k, :, x].astype(f32)
        for j in range(3):
            t = t + rx_b[k, j].astype(f32)
        s2_b[k] = t.astype(bf16)
        for cp in z_cp[k]:
            start(cp)

    agz_cp = [[copy(slab.at[k, h, z, x, c], slab.at[k, h, z, x, c], at(dh=a, dz=b)) for a, b in z8_offs] for k in range(2)]
    agx_cp = [[copy(slab.at[k, :, :, x, c], slab.at[k, :, :, x, c], at(dx=j)) for j in (1, 3, 2)] for k in range(2)]
    agc_cp = [copy(slab.at[k, :, :, :, c], slab.at[k, :, :, :, c], at(dc=1)) for k in range(2)]
    nz_cp = [[copy(nsrc.at[k, 0], nbuf.at[k, i], at(dh=a, dz=b)) for i, (a, b) in enumerate(z8_offs)] for k in range(2)]
    nx_cp = [[copy(nsrc.at[k, 1], nbuf.at[k, 7 + i], at(dx=j)) for i, j in enumerate((1, 3, 2))] for k in range(2)]
    nc_cp = [[copy(nsrc.at[k, 2], nbuf.at[k, 10], at(dc=1))] for k in range(2)]
    ny_cp = [[copy(nsrc.at[k, 3], nbuf.at[k, 11 + i], at(dy=j)) for i, j in enumerate((1, 3, 2))] for k in range(2)]

    def total(v):
        return jnp.broadcast_to(
            jnp.sum(jnp.sum(v, axis=0, keepdims=True), axis=1, keepdims=True), (8, 128))

    def gathered(k, cps, nst, first, n):
        for cp in cps:
            cp.wait_recv()
        t = nsrc[k, nst]
        for i in range(n):
            t = t + nbuf[k, first + i]
        nsrc[k, nst + 1] = t

    grad_part = copy(grad2.at[h], grad2.at[h], at(dh=1))
    gx_cp = [copy(gx.at[f], gx.at[f], at(dh=a, dy=b)) for a, b in fac_offs]

    def z_done(k):
        for cp in z_cp[k]:
            cp.wait_recv()
        t = s2_b[k, z].astype(f32)
        for j in range(3):
            t = t + rz_b[k, j].astype(f32)
        if k == 0:
            grad2[h] = t
            return t
        slab[k - 1, h, z, x, c] = t.astype(bf16)
        ri = d * R + lax.broadcasted_iota(jnp.int32, (R, B), 0)
        ci = f * B + lax.broadcasted_iota(jnp.int32, (R, B), 1)
        t = t + jnp.where(ri == ci, damping, 0.0)
        nsrc[k - 1, 0] = total(t * t)
        for cp in agz_cp[k - 1] + nz_cp[k - 1]:
            start(cp)
        return None

    def agz_done(k):
        gathered(k - 1, agz_cp[k - 1] + nz_cp[k - 1], 0, 0, 7)
        for cp in agx_cp[k - 1] + nx_cp[k - 1]:
            start(cp)

    def agx_done(k):
        gathered(k - 1, agx_cp[k - 1] + nx_cp[k - 1], 1, 7, 3)
        for cp in [agc_cp[k - 1]] + nc_cp[k - 1]:
            start(cp)

    def agc_done(k):
        gathered(k - 1, [agc_cp[k - 1]] + nc_cp[k - 1], 2, 10, 1)
        for cp in ny_cp[k - 1]:
            start(cp)

    def alpha_of(k):
        for cp in ny_cp[k - 1]:
            cp.wait_recv()
        t = nsrc[k - 1, 3]
        for i in range(3):
            t = t + nbuf[k - 1, 11 + i]
        return (1.0 / jnp.sqrt(t))[0:1, 0:1]

    def slab_rows(k, e, b):
        return slab[k - 1, e, b // 2, (b % 2) * 2:(b % 2) * 2 + 2].reshape(B, B)

    def both(k, block):
        cols = []
        for e in range(2):
            t = dot(block(0), slab_rows(k, e, 0))
            for b in range(1, 8):
                t = t + dot(block(b), slab_rows(k, e, b))
            cols.append(t)
        return jnp.concatenate(cols, axis=1)

    x_own = [None] * 6
    step_cp = [[copy(xg.at[i, y], xg.at[i, y], at(dy=j)) for j in (2, 1, 3)] for i in range(6)]

    def step_send(i, value):
        v = value.astype(bf16)
        xg[i, y, 0] = v[:, :B]
        xg[i, y, 1] = v[:, B:]
        x_own[i] = value
        for cp in step_cp[i]:
            start(cp)

    def step_mul(i, k):
        for cp in step_cp[i]:
            cp.wait_recv()
        return x_own[i] * damping + both(k, lambda b: xg[i, b % 4, b // 4])

    t_base = []
    for _ in range(2):
        t_base.append(count[0])
        count[0] += 8
    t_slot = (fd // 4) * 4 + d % 4

    def t_copy(i, e, m, slot):
        if i == 0:
            dev = {"dp": 4 * f + m, "fac": e * 4 + fd % 4}
        else:
            dev = {"dp": 4 * (e * 4 + y) + m, "fac": h * 4 + fd % 4}
        return pltpu.make_async_remote_copy(
            src_ref=tsrc.at[i, 0 if i == 0 else e, m // 2], dst_ref=tdst.at[i, slot],
            send_sem=ssem.at[t_base[i] + e * 4 + m], recv_sem=rsem.at[t_base[i] + slot],
            device_id=dev, device_id_type=pl.DeviceIdType.MESH)

    def t_here(i, e, m):
        if i == 0:
            return own0 & (d == 4 * f + m) & (h == e)
        return own1 & (d == 4 * (e * 4 + y) + m)

    def t_send(i, value):
        for e in range(value.shape[1] // B):
            for q in range(2):
                tsrc[i, e, q] = value[:, e * B + q * 128:e * B + (q + 1) * 128]
        for e in range(2):
            for m in range(4):
                here = t_here(i, e, m)

                @pl.when(here)
                def _(e=e, m=m):
                    pltpu.make_async_copy(
                        tsrc.at[i, 0 if i == 0 else e, m // 2], tdst.at[i, t_slot],
                        rsem.at[t_base[i] + t_slot]).start()

                @pl.when(jnp.logical_not(here))
                def _(e=e, m=m):
                    t_copy(i, e, m, t_slot).start()

    def t_recv(i):
        for k in range(8):
            t_copy(i, k // 4, k % 4, k).wait_recv()
        for e in range(2):
            s = jnp.concatenate([tdst[i, e * 4 + k] for k in range(4)], axis=0)
            tt[:, e * B:(e + 1) * B] = s.T
        return tt[pl.ds(pl.multiple_of((d % 2) * R, R), R), :]

    lax.fori_loop(0, TOK // 32, norm, 0)
    gram(1, n_all, n_all)
    start(core_cp[1])
    g_cot.middle()
    for cp in w_cps:
        cp.wait_recv()
    start(w_core)
    core_done(1)
    g_cot.finish_a()
    g_cot.finish_b()
    w_core.wait_recv()

    acc[...] = jnp.zeros_like(acc)

    def og(b, _):
        w_blk = w_all[pl.ds(b * 2, 2)].reshape(B, B)
        acc[...] += dot(cot_all[b], w_blk)
        return 0

    lax.fori_loop(0, 8, og, 0)
    for s in range(2):
        rows = pl.ds(s * ORBS, ORBS)
        og_s = (acc[rows, :] * keep_s[rows, :]).astype(bf16)
        for hd in range(2):
            v = dot_t(probs[s, hd], og_s[:, hd * 128:(hd + 1) * 128])
            v_all[f, rows, pl.ds(hd * 128, 128)] = v.astype(bf16)
    g_v.begin_z()
    g_v.begin_y()
    gram(0, n_all, v_all)
    start(core_cp[0])
    x_done(1)
    core_done(0)
    z_done(1)
    g_v.middle()
    x_done(0)
    agz_done(1)
    g_v.finish_a()
    g_v.finish_b()
    gram(2, v_all, v_all)
    start(core_cp[2])
    grad = z_done(0)
    t_send(0, grad)
    gx[f] = grad.astype(bf16)
    for cp in gx_cp + [grad_part]:
        start(cp)
    core_done(2)
    agx_done(1)
    x0 = t_recv(0)
    step_send(0, x0)
    agc_done(1)
    x_done(2)
    a_alpha = alpha_of(1)
    c1 = 4.0 * x0 - a_alpha * step_mul(0, 1)
    step_send(1, c1)
    z_done(2)
    c2 = 6.0 * x0 - a_alpha * step_mul(1, 1)
    step_send(2, c2)
    agz_done(2)
    c3 = 4.0 * x0 - a_alpha * step_mul(2, 1)
    t_send(1, c3)
    agx_done(2)
    l0 = t_recv(1)
    step_send(3, l0)
    for cp in gx_cp + [grad_part]:
        cp.wait_recv()
    agc_done(2)
    q0 = both(2, lambda b: gx[b])
    g_alpha = alpha_of(2)
    grads = jnp.concatenate([grad2[0], grad2[1]], axis=1)
    q0 = q0 + damping * grads
    c1 = 4.0 * l0 - g_alpha * step_mul(3, 2)
    step_send(4, c1)
    c2 = 6.0 * l0 - g_alpha * step_mul(4, 2)
    step_send(5, c2)

    fin[0] = total(4.0 * grads * l0 - g_alpha * (q0 * c2))
    fc = start(copy(fin.at[0], fin.at[1], at(dc=1)))
    fx = [copy(fin.at[2], fin.at[3 + i], at(dz=a, dx=b)) for i, (a, b) in enumerate(dp_offs)]
    fy = [copy(fin.at[18], fin.at[19 + i], at(dy=j)) for i, j in enumerate((2, 1, 3))]
    fc.wait_recv()
    fin[2] = fin[0] + fin[1]
    for cp in fx:
        start(cp)
    c3 = 4.0 * l0 - g_alpha * step_mul(5, 2)
    ab = a_alpha * g_alpha
    for cp in fx:
        cp.wait_recv()
    t = fin[2]
    for i in range(15):
        t = t + fin[3 + i]
    fin[18] = t
    for cp in fy:
        start(cp)
    tt[0:R, :] = c3 * ab
    for cp in fy:
        cp.wait_recv()
    for i in range(3):
        t = t + fin[19 + i]
    inner = t[0:1, 0:1] * ab
    out[...] = tt[0:R, pl.ds(pl.multiple_of(h * B, B), B)] * (float(D) / jnp.sqrt(inner + epsilon))

    for cp in started:
        cp.wait_send()
    for i in range(2):
        for e in range(2):
            for m in range(4):
                @pl.when(jnp.logical_not(t_here(i, e, m)))
                def _(i=i, e=e, m=m):
                    t_copy(i, e, m, 0).wait_send()
    assert count[0] <= NSEM


def per_device(occupations, stream, norm_gain, probs, w_out, cotangent):
    vm = pl.BlockSpec(memory_space=pltpu.VMEM)
    hb = pl.BlockSpec(memory_space=pl.ANY)
    V = pltpu.VMEM
    return pl.pallas_call(
        kernel,
        out_shape=jax.ShapeDtypeStruct((R, B), f32),
        in_specs=[vm, hb, vm, hb, hb, hb],
        out_specs=vm,
        scratch_shapes=[
            V((8, TOK, B), bf16),
            V((8, TOK, B), bf16),
            V((8, TOK, B), bf16),
            V((8, TOK, B), bf16),
            V((16, 2, R, B), bf16),
            V((2, 2, ORBS, ORBS), bf16),
            V((TOK, B), f32),
            V((TOK, 1), f32),
            V((3, 16, 2, R, B), bf16),
            V((3, 16, R, B), bf16),
            V((3, 4, 4, R, B), bf16),
            V((3, 3, 4, R, B), bf16),
            V((3, 4, R, B), bf16),
            V((3, 3, R, B), bf16),
            V((2, 2, 4, 4, 2, R, B), bf16),
            V((2, R, B), f32),
            V((8, R, B), bf16),
            V((2, 2, 2, R, 128), f32),
            V((2, 8, R, 128), f32),
            V((128, 2 * B), f32),
            V((6, 4, 2, R, B), bf16),
            V((2, 4, 8, 128), f32),
            V((2, 14, 8, 128), f32),
            V((22, 8, 128), f32),
            pltpu.SemaphoreType.DMA((4,)),
            pltpu.SemaphoreType.DMA((NSEM,)),
            pltpu.SemaphoreType.DMA((NSEM,)),
        ],
        compiler_params=pltpu.CompilerParams(
            collective_id=0, has_side_effects=True, vmem_limit_bytes=56 << 20),
    )(occupations, stream, norm_gain.reshape(1, D), probs, w_out.T, cotangent)


def solution(mesh):
    placed = (
        P("dp", None),
        P("dp", "fac"),
        P(),
        P("dp", "fac", None, None),
        P("fac", "dp"),
        P("dp", "fac"),
    )
    return jax.shard_map(
        per_device, mesh=mesh, in_specs=placed, out_specs=P("dp", "fac"), check_vma=False
    )
```

```python
import jax
import jax.numpy as jnp
from jax import lax
from jax.experimental import pallas as pl
from jax.experimental.pallas import tpu as pltpu
from jax.sharding import PartitionSpec as P

ORBS = 256
NE = 48
TOK = 512
D = 2048
B = 256
R = 64
SCALE = 1.0 / 16384
damping = 0.1
epsilon = 1e-06
bf16 = jnp.bfloat16
f32 = jnp.float32
NSEM = 240


def dot(a, b):
    return lax.dot_general(a, b, (((1,), (0,)), ((), ())), preferred_element_type=f32)


def dot_t(a, b):
    return lax.dot_general(a, b, (((0,), (0,)), ((), ())), preferred_element_type=f32)


def kernel(occ, stream_h, gain, probs_h, w_h, cot_h, out,
           cot_all, st_all, n_all, v_all, w_all, probs, acc, keep_s,
           part, rc_b, s1_b, rx_b, s2_b, rz_b, slab,
           grad2, gx, tp, tpo, tsrc, tdst, tt, xg, nsrc, nbuf, fin, lsem, ssem, rsem):
    d = lax.axis_index("dp")
    f = lax.axis_index("fac")
    z, x, c = d // 8, (d // 2) % 4, d % 2
    h, y = f // 4, f % 4
    fd = d // 4
    mesh_id = pl.DeviceIdType.MESH

    def at(dh=0, dy=0, dz=0, dx=0, dc=0):
        nd = (((z + dz) % 4) * 4 + (x + dx) % 4) * 2 + (c + dc) % 2
        nf = ((h + dh) % 2) * 4 + (y + dy) % 4
        return {"dp": nd, "fac": nf}

    count = [0]
    started = []

    def copy(src, dst, dev):
        i = count[0]
        count[0] += 1
        return pltpu.make_async_remote_copy(
            src_ref=src, dst_ref=dst, send_sem=ssem.at[i], recv_sem=rsem.at[i],
            device_id=dev, device_id_type=pl.DeviceIdType.MESH)

    def start(cp):
        cp.start()
        started.append(cp)
        return cp

    fac_offs = [(1, 2), (1, 1), (1, 3), (1, 0), (0, 2), (0, 1), (0, 3)]
    dp_offs = [(a, b) for a in range(4) for b in range(4) if (a, b) != (0, 0)]
    z8_offs = [(1, 0), (1, 1), (1, 2), (1, 3), (0, 2), (0, 1), (0, 3)]

    bar = pltpu.get_barrier_semaphore()

    def greet(dev):
        pl.semaphore_signal(bar, inc=1, device_id=dev, device_id_type=mesh_id)

    for a, b in fac_offs:
        greet(at(dh=a, dy=b))
    for a, b in dp_offs:
        greet(at(dz=a, dx=b))
    greet(at(dc=1))
    for j in (1, 2, 3):
        greet(at(dh=1, dz=j))
    own0 = fd == f
    own1 = fd % 4 == y
    pair = x % 2
    for e in range(2):
        for kk in range(2):
            src_d = 4 * (e * 4 + y) + 2 * kk + pair

            @pl.when(jnp.logical_not(own0 & (d == src_d)))
            def _(src_d=src_d):
                greet({"dp": src_d, "fac": fd})

            @pl.when(jnp.logical_not(own1 & (d == src_d)))
            def _(src_d=src_d):
                greet({"dp": src_d, "fac": h * 4 + fd % 4})

    local = [pltpu.make_async_copy(a, b, lsem.at[i]) for i, (a, b) in enumerate([
        (stream_h, st_all.at[f]), (cot_h, cot_all.at[f]), (w_h, w_all.at[z * 4 + x, c]), (probs_h, probs)])]
    for cp in local:
        cp.start()
    pl.semaphore_wait(bar, 7 + 15 + 1 + 3 + 8 - (own0 & (pair == c)).astype(jnp.int32) - (own1 & (pair == c)).astype(jnp.int32))

    class Gather:
        def __init__(self, buf):
            other = (1 - h) * 4 + y
            self.buf = buf
            self.first = [self.piece(f, k, dict(dh=1)) for k in range(2)]
            self.ring = [[self.piece(f, 0, dict(dy=1)), self.piece(f, 1, dict(dy=3))],
                         [self.piece(f, 1, dict(dy=1)), self.piece(f, 0, dict(dy=3))]]
            self.fwd = [[self.piece(other, k, dict(dy=1)), self.piece(other, k, dict(dy=3))] for k in range(2)]
            self.hop = [[self.piece(e * 4 + (y + 3) % 4, 0, dict(dy=1)), self.piece(e * 4 + (y + 1) % 4, 1, dict(dy=3))]
                        for e in (h, 1 - h)]

        def piece(self, block, k, to):
            ref = self.buf.at[block, pl.ds(k * 256, 256)]
            return copy(ref, ref, at(**to))

        def begin_z(self):
            for cp in self.first:
                start(cp)

        def begin_y(self):
            for cp in self.ring[0] + self.ring[1]:
                start(cp)

        def ring_fwd(self):
            for i in range(2):
                self.ring[0][i].wait_recv()
                start(self.hop[0][i])

        def middle(self, k):
            self.first[k].wait_recv()
            for cp in self.fwd[k]:
                start(cp)

        def tail_fwd(self):
            self.fwd[0][0].wait_recv()
            start(self.hop[1][0])
            self.fwd[1][1].wait_recv()
            start(self.hop[1][1])

        def own_half(self):
            for cp in self.ring[1] + self.hop[0]:
                cp.wait_recv()

        def finish(self):
            for cp in [self.fwd[0][1], self.fwd[1][0]] + self.hop[1]:
                cp.wait_recv()

    g_st, g_cot, g_v = Gather(st_all), Gather(cot_all), Gather(v_all)
    local[0].wait()
    g_st.begin_z()
    g_st.begin_y()
    row = lax.broadcasted_iota(jnp.int32, (ORBS, ORBS), 0)
    col = lax.broadcasted_iota(jnp.int32, (ORBS, ORBS), 1)
    pos = lax.broadcasted_iota(jnp.int32, (ORBS, 1), 0).astype(f32)
    for s in range(2):
        ones = occ[pl.ds(s, 1), :].astype(f32)
        before = jnp.sum(jnp.where(col < row, ones, 0.0), axis=1, keepdims=True)
        forced = (before == float(NE)) | (pos - before == float(ORBS - NE))
        keep_s[pl.ds(s * ORBS, ORBS), :] = jnp.where(forced, 0.0, 1.0)
    for cp in local[1:]:
        cp.wait()
    g_st.ring_fwd()
    g_st.middle(0)
    g_st.middle(1)
    g_cot.begin_z()
    w_me = w_all.at[z * 4 + x, c]
    w_cps = [start(copy(w_me, w_me, at(dz=a, dx=b))) for a, b in dp_offs]
    w_core = copy(w_all.at[:, c], w_all.at[:, c], at(dc=1))
    g_st.own_half()
    g_st.tail_fwd()
    g_cot.begin_y()
    g_st.finish()

    def norm(t, _):
        rows = pl.ds(pl.multiple_of(t * 32, 32), 32)
        sq = jnp.zeros((32, B), f32)
        for b in range(8):
            v = st_all[b, rows, :].astype(f32)
            sq = sq + v * v
        inv = lax.rsqrt(jnp.sum(sq, axis=1, keepdims=True) * (1.0 / D) + epsilon)
        for b in range(8):
            v = st_all[b, rows, :].astype(f32)
            n_all[b, rows, :] = (v * inv * gain[:, b * B:(b + 1) * B]).astype(bf16)
        return 0

    def gram(k, left, right):
        def body(b, _):
            p = dot_t(left[b], right[f]) * SCALE
            part[k, pl.ds(b * 2, 2)] = p.astype(bf16).reshape(2, 2, R, B)
            return 0
        lax.fori_loop(0, 8, body, 0)

    core_cp = [copy(part.at[k, :, 1 - c], rc_b.at[k], at(dc=1)) for k in range(3)]
    x_cp = [[copy(s1_b.at[k, :, (x + j) % 4], rx_b.at[k, j - 1], at(dx=j)) for j in (1, 3, 2)] for k in range(3)]

    def core_done(k):
        core_cp[k].wait_recv()

        def body(q, _):
            s1_b[k, q] = (part[k, pl.ds(q * 4, 4), c].astype(f32)
                          + rc_b[k, pl.ds(q * 4, 4)].astype(f32)).astype(bf16)
            return 0
        lax.fori_loop(0, 4, body, 0)
        for cp in x_cp[k]:
            start(cp)

    z_cp = [[copy(s2_b.at[k, (z + j) % 4], rz_b.at[k, j - 1], at(dz=j)) for j in (2, 1, 3)] for k in range(3)]

    def x_done(k):
        for cp in x_cp[k]:
            cp.wait_recv()
        t = s1_b[k, :, x].astype(f32)
        for j in range(3):
            t = t + rx_b[k, j].astype(f32)
        s2_b[k] = t.astype(bf16)
        for cp in z_cp[k]:
            start(cp)

    agz_cp = [[copy(slab.at[k, h, z, x, c], slab.at[k, h, z, x, c], at(dh=a, dz=b)) for a, b in z8_offs] for k in range(2)]
    agx_cp = [[copy(slab.at[k, :, :, x, c], slab.at[k, :, :, x, c], at(dx=j)) for j in (1, 3, 2)] for k in range(2)]
    agc_cp = [copy(slab.at[k, :, :, :, c], slab.at[k, :, :, :, c], at(dc=1)) for k in range(2)]
    nz_cp = [[copy(nsrc.at[k, 0], nbuf.at[k, i], at(dh=a, dz=b)) for i, (a, b) in enumerate(z8_offs)] for k in range(2)]
    nx_cp = [[copy(nsrc.at[k, 1], nbuf.at[k, 7 + i], at(dx=j)) for i, j in enumerate((1, 3, 2))] for k in range(2)]
    nc_cp = [[copy(nsrc.at[k, 2], nbuf.at[k, 10], at(dc=1))] for k in range(2)]
    ny_cp = [[copy(nsrc.at[k, 3], nbuf.at[k, 11 + i], at(dy=j)) for i, j in enumerate((1, 3, 2))] for k in range(2)]

    def total(v):
        return jnp.broadcast_to(
            jnp.sum(jnp.sum(v, axis=0, keepdims=True), axis=1, keepdims=True), (8, 128))

    def gathered(k, cps, nst, first, n):
        for cp in cps:
            cp.wait_recv()
        t = nsrc[k, nst]
        for i in range(n):
            t = t + nbuf[k, first + i]
        nsrc[k, nst + 1] = t

    grad_part = copy(grad2.at[h], grad2.at[h], at(dh=1))
    gx_cp = [copy(gx.at[f], gx.at[f], at(dh=a, dy=b)) for a, b in fac_offs]

    def z_done(k):
        for cp in z_cp[k]:
            cp.wait_recv()
        t = s2_b[k, z].astype(f32)
        for j in range(3):
            t = t + rz_b[k, j].astype(f32)
        if k == 0:
            grad2[h] = t
            return t
        slab[k - 1, h, z, x, c] = t.astype(bf16)
        ri = d * R + lax.broadcasted_iota(jnp.int32, (R, B), 0)
        ci = f * B + lax.broadcasted_iota(jnp.int32, (R, B), 1)
        t = t + jnp.where(ri == ci, damping, 0.0)
        nsrc[k - 1, 0] = total(t * t)
        return None

    def agz_start(k):
        for cp in agz_cp[k - 1] + nz_cp[k - 1]:
            start(cp)

    def agz_done(k):
        gathered(k - 1, agz_cp[k - 1] + nz_cp[k - 1], 0, 0, 7)
        for cp in agx_cp[k - 1] + nx_cp[k - 1]:
            start(cp)

    def agx_done(k):
        gathered(k - 1, agx_cp[k - 1] + nx_cp[k - 1], 1, 7, 3)
        for cp in [agc_cp[k - 1]] + nc_cp[k - 1]:
            start(cp)

    def agc_done(k):
        gathered(k - 1, [agc_cp[k - 1]] + nc_cp[k - 1], 2, 10, 1)
        for cp in ny_cp[k - 1]:
            start(cp)

    def alpha_of(k):
        for cp in ny_cp[k - 1]:
            cp.wait_recv()
        t = nsrc[k - 1, 3]
        for i in range(3):
            t = t + nbuf[k - 1, 11 + i]
        return (1.0 / jnp.sqrt(t))[0:1, 0:1]

    def slab_rows(k, e, b):
        return slab[k - 1, e, b // 2, (b % 2) * 2:(b % 2) * 2 + 2].reshape(B, B)

    def both(k, block):
        cols = []
        for e in range(2):
            t = dot(block(0), slab_rows(k, e, 0))
            for b in range(1, 8):
                t = t + dot(block(b), slab_rows(k, e, b))
            cols.append(t)
        return jnp.concatenate(cols, axis=1)

    x_own = [None] * 6
    step_cp = [[copy(xg.at[i, y], xg.at[i, y], at(dy=j)) for j in (2, 1, 3)] for i in range(6)]

    def step_send(i, value):
        v = value.astype(bf16)
        xg[i, y, 0] = v[:, :B]
        xg[i, y, 1] = v[:, B:]
        x_own[i] = value
        for cp in step_cp[i]:
            start(cp)

    def step_mul(i, k):
        for cp in step_cp[i]:
            cp.wait_recv()
        return x_own[i] * damping + both(k, lambda b: xg[i, b % 4, b // 4])

    t_base = []
    for _ in range(2):
        t_base.append(count[0])
        count[0] += 4
    t_slot = (fd // 4) * 2 + pair
    t_pair = [copy(tpo.at[0, 0], tp.at[0, 0, c], at(dc=1)),
              copy(tpo.at[1], tp.at[1, :, c], at(dc=1))]

    def t_copy(i, e, m, slot):
        if i == 0:
            dev = {"dp": 4 * f + 2 * c + m, "fac": e * 4 + fd % 4}
        else:
            dev = {"dp": 4 * (e * 4 + y) + 2 * c + m, "fac": h * 4 + fd % 4}
        return pltpu.make_async_remote_copy(
            src_ref=tsrc.at[i, 0 if i == 0 else e, m], dst_ref=tdst.at[i, slot],
            send_sem=ssem.at[t_base[i] + e * 2 + m], recv_sem=rsem.at[t_base[i] + slot],
            device_id=dev, device_id_type=pl.DeviceIdType.MESH)

    def t_here(i, e, m):
        if i == 0:
            return own0 & (d == 4 * f + 2 * c + m) & (h == e)
        return own1 & (d == 4 * (e * 4 + y) + 2 * c + m)

    def t_core(i, value):
        for e in range(i + 1):
            lo = value[:, e * B:e * B + 128]
            hi = value[:, e * B + 128:(e + 1) * B]
            tp[i, e, c] = jnp.where(c == 0, lo, hi)
            tpo[i, e] = jnp.where(c == 0, hi, lo)
        start(t_pair[i])

    def t_send(i):
        t_pair[i].wait_recv()
        for e in range(i + 1):
            tsrc[i, e] = tp[i, e].reshape(128, 128).T.reshape(2, R, 128)
        for e in range(2):
            for m in range(2):
                here = t_here(i, e, m)

                @pl.when(here)
                def _(e=e, m=m):
                    pltpu.make_async_copy(
                        tsrc.at[i, 0 if i == 0 else e, m], tdst.at[i, t_slot],
                        rsem.at[t_base[i] + t_slot]).start()

                @pl.when(jnp.logical_not(here))
                def _(e=e, m=m):
                    t_copy(i, e, m, t_slot).start()

    def t_recv(i):
        for k in range(4):
            t_copy(i, k // 2, k % 2, k).wait_recv()
        return jnp.concatenate([tdst[i, k] for k in range(4)], axis=1)

    lax.fori_loop(0, TOK // 32, norm, 0)
    gram(1, n_all, n_all)
    start(core_cp[1])
    g_cot.ring_fwd()
    core_done(1)
    for cp in w_cps:
        cp.wait_recv()
    start(w_core)
    g_cot.middle(0)
    g_cot.middle(1)
    g_cot.own_half()
    g_cot.tail_fwd()
    x_done(1)
    g_cot.finish()
    w_core.wait_recv()

    acc[...] = jnp.zeros_like(acc)

    def og(b, _):
        w_blk = w_all[pl.ds(b * 2, 2)].reshape(B, B)
        acc[...] += dot(cot_all[b], w_blk)
        return 0

    lax.fori_loop(0, 8, og, 0)
    for s in range(2):
        rows = pl.ds(s * ORBS, ORBS)
        og_s = (acc[rows, :] * keep_s[rows, :]).astype(bf16)
        for hd in range(2):
            v = dot_t(probs[s, hd], og_s[:, hd * 128:(hd + 1) * 128])
            v_all[f, rows, pl.ds(hd * 128, 128)] = v.astype(bf16)
    g_v.begin_z()
    g_v.begin_y()
    gram(0, n_all, v_all)
    start(core_cp[0])
    z_done(1)
    agz_start(1)
    core_done(0)
    g_v.ring_fwd()
    g_v.middle(0)
    g_v.middle(1)
    x_done(0)
    g_v.own_half()
    g_v.tail_fwd()
    agz_done(1)
    grad = z_done(0)
    t_core(0, grad)
    gx[f] = grad.astype(bf16)
    t_send(0)
    g_v.finish()
    gram(2, v_all, v_all)
    start(core_cp[2])
    core_done(2)
    x0 = t_recv(0)
    step_send(0, x0)
    agx_done(1)
    x_done(2)
    agc_done(1)
    a_alpha = alpha_of(1)
    c1 = 4.0 * x0 - a_alpha * step_mul(0, 1)
    step_send(1, c1)
    z_done(2)
    agz_start(2)
    c2 = 6.0 * x0 - a_alpha * step_mul(1, 1)
    step_send(2, c2)
    agz_done(2)
    for cp in gx_cp + [grad_part]:
        start(cp)
    c3 = 4.0 * x0 - a_alpha * step_mul(2, 1)
    t_core(1, c3)
    t_send(1)
    agx_done(2)
    l0 = t_recv(1)
    step_send(3, l0)
    agc_done(2)
    g_alpha = alpha_of(2)
    c1 = 4.0 * l0 - g_alpha * step_mul(3, 2)
    step_send(4, c1)
    for cp in gx_cp + [grad_part]:
        cp.wait_recv()
    grads = jnp.concatenate([grad2[0], grad2[1]], axis=1)
    q0 = both(2, lambda b: gx[b]) + damping * grads
    c2 = 6.0 * l0 - g_alpha * step_mul(4, 2)
    step_send(5, c2)

    fin[0] = total(4.0 * grads * l0 - g_alpha * (q0 * c2))
    fc = start(copy(fin.at[0], fin.at[1], at(dc=1)))
    fx = [copy(fin.at[2], fin.at[3 + i], at(dz=a, dx=b)) for i, (a, b) in enumerate(dp_offs)]
    fy = [copy(fin.at[18], fin.at[19 + i], at(dy=j)) for i, j in enumerate((2, 1, 3))]
    fc.wait_recv()
    fin[2] = fin[0] + fin[1]
    for cp in fx:
        start(cp)
    c3 = 4.0 * l0 - g_alpha * step_mul(5, 2)
    ab = a_alpha * g_alpha
    for cp in fx:
        cp.wait_recv()
    t = fin[2]
    for i in range(15):
        t = t + fin[3 + i]
    fin[18] = t
    for cp in fy:
        start(cp)
    tt[0:R, :] = c3 * ab
    for cp in fy:
        cp.wait_recv()
    for i in range(3):
        t = t + fin[19 + i]
    inner = t[0:1, 0:1] * ab
    out[...] = tt[0:R, pl.ds(pl.multiple_of(h * B, B), B)] * (float(D) / jnp.sqrt(inner + epsilon))

    for cp in started:
        cp.wait_send()
    for i in range(2):
        for e in range(2):
            for m in range(2):
                @pl.when(jnp.logical_not(t_here(i, e, m)))
                def _(i=i, e=e, m=m):
                    t_copy(i, e, m, 0).wait_send()
    assert count[0] <= NSEM


def per_device(occupations, stream, norm_gain, probs, w_out, cotangent):
    vm = pl.BlockSpec(memory_space=pltpu.VMEM)
    hb = pl.BlockSpec(memory_space=pl.ANY)
    V = pltpu.VMEM
    return pl.pallas_call(
        kernel,
        out_shape=jax.ShapeDtypeStruct((R, B), f32),
        in_specs=[vm, hb, vm, hb, hb, hb],
        out_specs=vm,
        scratch_shapes=[
            V((8, TOK, B), bf16),
            V((8, TOK, B), bf16),
            V((8, TOK, B), bf16),
            V((8, TOK, B), bf16),
            V((16, 2, R, B), bf16),
            V((2, 2, ORBS, ORBS), bf16),
            V((TOK, B), f32),
            V((TOK, 1), f32),
            V((3, 16, 2, R, B), bf16),
            V((3, 16, R, B), bf16),
            V((3, 4, 4, R, B), bf16),
            V((3, 3, 4, R, B), bf16),
            V((3, 4, R, B), bf16),
            V((3, 3, R, B), bf16),
            V((2, 2, 4, 4, 2, R, B), bf16),
            V((2, R, B), f32),
            V((8, R, B), bf16),
            V((2, 2, 2, R, 128), f32),
            V((2, 2, R, 128), f32),
            V((2, 2, 2, R, 128), f32),
            V((2, 4, R, 128), f32),
            V((R, 2 * B), f32),
            V((6, 4, 2, R, B), bf16),
            V((2, 4, 8, 128), f32),
            V((2, 14, 8, 128), f32),
            V((22, 8, 128), f32),
            pltpu.SemaphoreType.DMA((4,)),
            pltpu.SemaphoreType.DMA((NSEM,)),
            pltpu.SemaphoreType.DMA((NSEM,)),
        ],
        compiler_params=pltpu.CompilerParams(
            collective_id=0, has_side_effects=True, vmem_limit_bytes=56 << 20),
    )(occupations, stream, norm_gain.reshape(1, D), probs, w_out.T, cotangent)


def solution(mesh):
    placed = (
        P("dp", None),
        P("dp", "fac"),
        P(),
        P("dp", "fac", None, None),
        P("fac", "dp"),
        P("dp", "fac"),
    )
    return jax.shard_map(
        per_device, mesh=mesh, in_specs=placed, out_specs=P("dp", "fac"), check_vma=False
    )
```

```python
import jax
import jax.numpy as jnp
from jax import lax
from jax.experimental import pallas as pl
from jax.experimental.pallas import tpu as pltpu
from jax.sharding import PartitionSpec as P

ORBS = 256
NE = 48
TOK = 512
D = 2048
B = 256
R = 64
SCALE = 1.0 / 16384
damping = 0.1
epsilon = 1e-06
bf16 = jnp.bfloat16
f32 = jnp.float32
NSEM = 240


def dot(a, b):
    return lax.dot_general(a, b, (((1,), (0,)), ((), ())), preferred_element_type=f32)


def dot_t(a, b):
    return lax.dot_general(a, b, (((0,), (0,)), ((), ())), preferred_element_type=f32)


def kernel(occ, stream_h, gain, probs_h, w_h, cot_h, out,
           cot_all, st_all, n_all, v_all, w_all, probs, acc, keep_s,
           part, part_f, s1_f, s2_f, rc_b, s1_b, rx_b, s2_b, rz_b, slab, s2g, rzg,
           grad2, gx, tp, tpo, tsrc, tdst, tt, xg, nsrc, nbuf, fin, lsem, ssem, rsem):
    d = lax.axis_index("dp")
    f = lax.axis_index("fac")
    z, x, c = d // 8, (d // 2) % 4, d % 2
    h, y = f // 4, f % 4
    fd = d // 4
    mesh_id = pl.DeviceIdType.MESH

    def at(dh=0, dy=0, dz=0, dx=0, dc=0):
        nd = (((z + dz) % 4) * 4 + (x + dx) % 4) * 2 + (c + dc) % 2
        nf = ((h + dh) % 2) * 4 + (y + dy) % 4
        return {"dp": nd, "fac": nf}

    count = [0]
    started = []

    def copy(src, dst, dev):
        i = count[0]
        count[0] += 1
        return pltpu.make_async_remote_copy(
            src_ref=src, dst_ref=dst, send_sem=ssem.at[i], recv_sem=rsem.at[i],
            device_id=dev, device_id_type=pl.DeviceIdType.MESH)

    def start(cp):
        cp.start()
        started.append(cp)
        return cp

    fac_offs = [(1, 2), (1, 1), (1, 3), (1, 0), (0, 2), (0, 1), (0, 3)]
    dp_offs = [(a, b) for a in range(4) for b in range(4) if (a, b) != (0, 0)]
    z8_offs = [(1, 0), (1, 1), (1, 2), (1, 3), (0, 2), (0, 1), (0, 3)]

    bar = pltpu.get_barrier_semaphore()

    def greet(dev):
        pl.semaphore_signal(bar, inc=1, device_id=dev, device_id_type=mesh_id)

    for a, b in fac_offs:
        greet(at(dh=a, dy=b))
    for a, b in dp_offs:
        greet(at(dz=a, dx=b))
    greet(at(dc=1))
    for j in (1, 2, 3):
        greet(at(dh=1, dz=j))
    own0 = fd == f
    own1 = fd % 4 == y
    pair = x % 2
    for e in range(2):
        for kk in range(2):
            src_d = 4 * (e * 4 + y) + 2 * kk + pair

            @pl.when(jnp.logical_not(own0 & (d == src_d)))
            def _(src_d=src_d):
                greet({"dp": src_d, "fac": fd})

            @pl.when(jnp.logical_not(own1 & (d == src_d)))
            def _(src_d=src_d):
                greet({"dp": src_d, "fac": h * 4 + fd % 4})

    local = [pltpu.make_async_copy(a, b, lsem.at[i]) for i, (a, b) in enumerate([
        (stream_h, st_all.at[f]), (cot_h, cot_all.at[f]), (w_h, w_all.at[z, x, c]), (probs_h, probs)])]
    for cp in local:
        cp.start()
    pl.semaphore_wait(bar, 7 + 15 + 1 + 3 + 8 - (own0 & (pair == c)).astype(jnp.int32) - (own1 & (pair == c)).astype(jnp.int32))

    class Gather:
        def __init__(self, buf):
            other = (1 - h) * 4 + y
            self.buf = buf
            self.first = [self.piece(f, k, dict(dh=1)) for k in range(2)]
            self.ring = [[self.piece(f, 0, dict(dy=1)), self.piece(f, 1, dict(dy=3))],
                         [self.piece(f, 1, dict(dy=1)), self.piece(f, 0, dict(dy=3))]]
            self.fwd = [[self.piece(other, k, dict(dy=1)), self.piece(other, k, dict(dy=3))] for k in range(2)]
            self.hop = [[self.piece(e * 4 + (y + 3) % 4, 0, dict(dy=1)), self.piece(e * 4 + (y + 1) % 4, 1, dict(dy=3))]
                        for e in (h, 1 - h)]

        def piece(self, block, k, to):
            ref = self.buf.at[block, pl.ds(k * 256, 256)]
            return copy(ref, ref, at(**to))

        def begin_z(self):
            for cp in self.first:
                start(cp)

        def begin_y(self):
            for cp in self.ring[0] + self.ring[1]:
                start(cp)

        def ring_fwd(self):
            for i in range(2):
                self.ring[0][i].wait_recv()
                start(self.hop[0][i])

        def middle(self, k):
            self.first[k].wait_recv()
            for cp in self.fwd[k]:
                start(cp)

        def tail_fwd(self):
            self.fwd[0][0].wait_recv()
            start(self.hop[1][0])
            self.fwd[1][1].wait_recv()
            start(self.hop[1][1])

        def own_half(self):
            for cp in self.ring[1] + self.hop[0]:
                cp.wait_recv()

        def finish(self):
            for cp in [self.fwd[0][1], self.fwd[1][0]] + self.hop[1]:
                cp.wait_recv()

    g_st, g_cot, g_v = Gather(st_all), Gather(cot_all), Gather(v_all)
    local[0].wait()
    g_st.begin_z()
    g_st.begin_y()
    row = lax.broadcasted_iota(jnp.int32, (ORBS, ORBS), 0)
    col = lax.broadcasted_iota(jnp.int32, (ORBS, ORBS), 1)
    pos = lax.broadcasted_iota(jnp.int32, (ORBS, 1), 0).astype(f32)
    for s in range(2):
        ones = occ[pl.ds(s, 1), :].astype(f32)
        before = jnp.sum(jnp.where(col < row, ones, 0.0), axis=1, keepdims=True)
        forced = (before == float(NE)) | (pos - before == float(ORBS - NE))
        keep_s[pl.ds(s * ORBS, ORBS), :] = jnp.where(forced, 0.0, 1.0)
    for cp in local[1:]:
        cp.wait()
    w_z = [copy(w_all.at[z, x, c], w_all.at[z, x, c], at(dz=j)) for j in (2, 1, 3)]
    w_x = [copy(w_all.at[:, x, c], w_all.at[:, x, c], at(dx=j)) for j in (1, 3, 2)]
    w_core = copy(w_all.at[:, :, c], w_all.at[:, :, c], at(dc=1))
    for cp in w_z:
        start(cp)
    g_st.ring_fwd()
    g_st.middle(0)
    g_st.middle(1)
    g_cot.begin_z()
    for cp in w_z:
        cp.wait_recv()
    for cp in w_x:
        start(cp)
    g_st.tail_fwd()
    g_cot.begin_y()
    g_st.own_half()
    g_st.finish()

    def norm(t, _):
        rows = pl.ds(pl.multiple_of(t * 32, 32), 32)
        sq = jnp.zeros((32, B), f32)
        for b in range(8):
            v = st_all[b, rows, :].astype(f32)
            sq = sq + v * v
        inv = lax.rsqrt(jnp.sum(sq, axis=1, keepdims=True) * (1.0 / D) + epsilon)
        for b in range(8):
            v = st_all[b, rows, :].astype(f32)
            n_all[b, rows, :] = (v * inv * gain[:, b * B:(b + 1) * B]).astype(bf16)
        return 0

    def gram(k, left, right):
        def body(b, _):
            p = dot_t(left[b], right[f]) * SCALE
            part[k, pl.ds(b * 2, 2)] = p.astype(bf16).reshape(2, 2, R, B)
            if k == 0:
                part_f[pl.ds(b * 2, 2)] = p.reshape(2, 2, R, B)
            return 0
        lax.fori_loop(0, 8, body, 0)

    core_cp = [copy(part.at[k, :, 1 - c], rc_b.at[k], at(dc=1)) for k in range(2)]
    x_cp = [[copy(s1_b.at[k, :, (x + j) % 4], rx_b.at[k, j - 1], at(dx=j)) for j in (1, 3, 2)] for k in range(2)]

    def core_done(k):
        core_cp[k].wait_recv()

        def body(q, _):
            mine = part_f[pl.ds(q * 4, 4), c] if k == 0 else part[k, pl.ds(q * 4, 4), c].astype(f32)
            t = mine + rc_b[k, pl.ds(q * 4, 4)].astype(f32)
            s1_b[k, q] = t.astype(bf16)
            if k == 0:
                s1_f[q] = t
            return 0
        lax.fori_loop(0, 4, body, 0)
        for cp in x_cp[k]:
            start(cp)

    z_cp = [[copy(s2_b.at[k, (z + j) % 4], rz_b.at[k, j - 1], at(dz=j)) for j in (2, 1, 3)] for k in range(2)]

    def x_done(k):
        for cp in x_cp[k]:
            cp.wait_recv()
        t = s1_f[:, x] if k == 0 else s1_b[k, :, x].astype(f32)
        for j in range(3):
            t = t + rx_b[k, j].astype(f32)
        s2_b[k] = t.astype(bf16)
        if k == 0:
            s2_f[...] = t
        for cp in z_cp[k]:
            start(cp)

    agz_cp = [copy(slab.at[0, h, z, x, c], slab.at[0, h, z, x, c], at(dh=a, dz=b)) for a, b in z8_offs]
    agx_cp = [copy(slab.at[0, :, :, x, c], slab.at[0, :, :, x, c], at(dx=j)) for j in (1, 3, 2)]
    agc_cp = copy(slab.at[0, :, :, :, c], slab.at[0, :, :, :, c], at(dc=1))
    nz_cp = [[copy(nsrc.at[k, 0], nbuf.at[k, i], at(dh=a, dz=b)) for i, (a, b) in enumerate(z8_offs)] for k in range(2)]
    nx_cp = [[copy(nsrc.at[k, 1], nbuf.at[k, 7 + i], at(dx=j)) for i, j in enumerate((1, 3, 2))] for k in range(2)]
    nc_cp = [[copy(nsrc.at[k, 2], nbuf.at[k, 10], at(dc=1))] for k in range(2)]
    ny_cp = [[copy(nsrc.at[k, 3], nbuf.at[k, 11 + i], at(dy=j)) for i, j in enumerate((1, 3, 2))] for k in range(2)]

    def total(v):
        return jnp.broadcast_to(
            jnp.sum(jnp.sum(v, axis=0, keepdims=True), axis=1, keepdims=True), (8, 128))

    def gathered(k, cps, nst, first, n):
        for cp in cps:
            cp.wait_recv()
        t = nsrc[k, nst]
        for i in range(n):
            t = t + nbuf[k, first + i]
        nsrc[k, nst + 1] = t

    grad_part = copy(grad2.at[h], grad2.at[h], at(dh=1))
    gx_cp = [copy(gx.at[f], gx.at[f], at(dh=a, dy=b)) for a, b in fac_offs]

    def z_done(k):
        for cp in z_cp[k]:
            cp.wait_recv()
        t = s2_f[z] if k == 0 else s2_b[k, z].astype(f32)
        for j in range(3):
            t = t + rz_b[k, j].astype(f32)
        if k == 0:
            grad2[h] = t
            return t
        slab[0, h, z, x, c] = t.astype(bf16).reshape(2, R // 2, B)
        ri = d * R + lax.broadcasted_iota(jnp.int32, (R, B), 0)
        ci = f * B + lax.broadcasted_iota(jnp.int32, (R, B), 1)
        t = t + jnp.where(ri == ci, damping, 0.0)
        nsrc[k - 1, 0] = total(t * t)
        return None

    def agz_start():
        for cp in agz_cp + nz_cp[0]:
            start(cp)

    def agz_done():
        gathered(0, agz_cp + nz_cp[0], 0, 0, 7)
        for cp in agx_cp + nx_cp[0]:
            start(cp)

    def agx_done():
        gathered(0, agx_cp + nx_cp[0], 1, 7, 3)
        for cp in [agc_cp] + nc_cp[0]:
            start(cp)

    def agc_done():
        gathered(0, [agc_cp] + nc_cp[0], 2, 10, 1)
        for cp in ny_cp[0]:
            start(cp)

    class Half:
        def __init__(self, q):
            self.q = q
            hh = h if q == 0 else 1 - h
            self.hh = hh
            self.planes = pl.ds(2 * hh, 2)
            rows = pl.ds(8 * hh, 8)
            self.core = copy(part.at[2, rows, 1 - c], rc_b.at[2, rows], at(dc=1))
            self.xs = [copy(s1_b.at[2, self.planes, (x + j) % 4], rx_b.at[2, j - 1, self.planes], at(dx=j)) for j in (1, 3, 2)]
            self.zs = [copy(s2g.at[q, (z + j) % 4], rzg.at[q, j - 1], at(dz=j)) for j in (2, 1, 3)]
            own_piece = slab.at[1, h, 2 * hh + z // 2, x, c, z % 2]
            self.agz = [copy(own_piece, own_piece, at(dh=a, dz=b)) for a, b in z8_offs]
            regions = [(e, 2 * e if q == 0 else 2 * (1 - e)) for e in range(2)]
            self.agx = [copy(slab.at[1, e, r:r + 2, x, c], slab.at[1, e, r:r + 2, x, c], at(dx=j))
                        for j in (1, 3, 2) for e, r in regions]
            self.agc = [copy(slab.at[1, e, r:r + 2, :, c], slab.at[1, e, r:r + 2, :, c], at(dc=1)) for e, r in regions]

        def gram(self):
            def body(i, _):
                b = self.hh * 4 + i
                p = dot_t(v_all[b], v_all[f]) * SCALE
                part[2, pl.ds(b * 2, 2)] = p.astype(bf16).reshape(2, 2, R, B)
                return 0
            lax.fori_loop(0, 4, body, 0)
            start(self.core)

        def core_done(self):
            self.core.wait_recv()

            def body(i, _):
                q = 2 * self.hh + i
                s1_b[2, q] = (part[2, pl.ds(q * 4, 4), c].astype(f32)
                              + rc_b[2, pl.ds(q * 4, 4)].astype(f32)).astype(bf16)
                return 0
            lax.fori_loop(0, 2, body, 0)
            for cp in self.xs:
                start(cp)

        def x_done(self):
            for cp in self.xs:
                cp.wait_recv()
            t = s1_b[2, self.planes, x].astype(f32)
            for j in range(3):
                t = t + rx_b[2, j, self.planes].astype(f32)
            s2g[self.q] = t.astype(bf16).reshape(4, R // 2, B)
            for cp in self.zs:
                start(cp)

        def z_done(self):
            for cp in self.zs:
                cp.wait_recv()
            t = s2g[self.q, z].astype(f32)
            for j in range(3):
                t = t + rzg[self.q, j].astype(f32)
            slab[1, h, 2 * self.hh + z // 2, x, c, z % 2] = t.astype(bf16)
            first = ((2 * self.hh + z // 2) * 8 + x * 2 + c) * R + (z % 2) * (R // 2)
            ri = first + lax.broadcasted_iota(jnp.int32, (R // 2, B), 0)
            ci = f * B + lax.broadcasted_iota(jnp.int32, (R // 2, B), 1)
            t = t + jnp.where(ri == ci, damping, 0.0)
            if self.q == 0:
                nsrc[1, 0] = total(t * t)
            else:
                nsrc[1, 0] += total(t * t)
            for cp in self.agz + (nz_cp[1] if self.q else []):
                start(cp)

        def agz_done(self):
            if self.q:
                gathered(1, self.agz + nz_cp[1], 0, 0, 7)
            else:
                for cp in self.agz:
                    cp.wait_recv()
            for cp in self.agx + (nx_cp[1] if self.q else []):
                start(cp)

        def agx_done(self):
            if self.q:
                gathered(1, self.agx + nx_cp[1], 1, 7, 3)
            else:
                for cp in self.agx:
                    cp.wait_recv()
            for cp in self.agc + (nc_cp[1] if self.q else []):
                start(cp)

        def agc_done(self):
            if self.q:
                gathered(1, self.agc + nc_cp[1], 2, 10, 1)
                for cp in ny_cp[1]:
                    start(cp)
            else:
                for cp in self.agc:
                    cp.wait_recv()

    ga, gb = Half(0), Half(1)

    def alpha_of(k):
        for cp in ny_cp[k - 1]:
            cp.wait_recv()
        t = nsrc[k - 1, 3]
        for i in range(3):
            t = t + nbuf[k - 1, 11 + i]
        return (1.0 / jnp.sqrt(t))[0:1, 0:1]

    def slab_rows(k, e, b):
        return slab[k - 1, e, b // 2, (b % 2) * 2:(b % 2) * 2 + 2].reshape(B, B)

    def both(k, block):
        cols = []
        for e in range(2):
            t = dot(block(0), slab_rows(k, e, 0))
            for b in range(1, 8):
                t = t + dot(block(b), slab_rows(k, e, b))
            cols.append(t)
        return jnp.concatenate(cols, axis=1)

    x_own = [None] * 6
    step_cp = [[copy(xg.at[i, y], xg.at[i, y], at(dy=j)) for j in (2, 1, 3)] for i in range(6)]

    def step_send(i, value):
        v = value.astype(bf16)
        xg[i, y, 0] = v[:, :B]
        xg[i, y, 1] = v[:, B:]
        x_own[i] = value
        for cp in step_cp[i]:
            start(cp)

    def step_mul(i, k):
        for cp in step_cp[i]:
            cp.wait_recv()
        return x_own[i] * damping + both(k, lambda b: xg[i, b % 4, b // 4])

    t_base = []
    for _ in range(2):
        t_base.append(count[0])
        count[0] += 4
    t_slot = (fd // 4) * 2 + pair
    t_pair = [copy(tpo.at[0, 0], tp.at[0, 0, c], at(dc=1)),
              copy(tpo.at[1], tp.at[1, :, c], at(dc=1))]

    def t_copy(i, e, m, slot):
        if i == 0:
            dev = {"dp": 4 * f + 2 * c + m, "fac": e * 4 + fd % 4}
        else:
            dev = {"dp": 4 * (e * 4 + y) + 2 * c + m, "fac": h * 4 + fd % 4}
        return pltpu.make_async_remote_copy(
            src_ref=tsrc.at[i, 0 if i == 0 else e, m], dst_ref=tdst.at[i, slot],
            send_sem=ssem.at[t_base[i] + e * 2 + m], recv_sem=rsem.at[t_base[i] + slot],
            device_id=dev, device_id_type=pl.DeviceIdType.MESH)

    def t_here(i, e, m):
        if i == 0:
            return own0 & (d == 4 * f + 2 * c + m) & (h == e)
        return own1 & (d == 4 * (e * 4 + y) + 2 * c + m)

    def t_core(i, value):
        for e in range(i + 1):
            lo = value[:, e * B:e * B + 128]
            hi = value[:, e * B + 128:(e + 1) * B]
            tp[i, e, c] = jnp.where(c == 0, lo, hi)
            tpo[i, e] = jnp.where(c == 0, hi, lo)
        start(t_pair[i])

    def t_send(i):
        t_pair[i].wait_recv()
        for e in range(i + 1):
            tsrc[i, e] = tp[i, e].reshape(128, 128).T.astype(bf16).reshape(2, R, 128)
        for e in range(2):
            for m in range(2):
                here = t_here(i, e, m)

                @pl.when(here)
                def _(e=e, m=m):
                    pltpu.make_async_copy(
                        tsrc.at[i, 0 if i == 0 else e, m], tdst.at[i, t_slot],
                        rsem.at[t_base[i] + t_slot]).start()

                @pl.when(jnp.logical_not(here))
                def _(e=e, m=m):
                    t_copy(i, e, m, t_slot).start()

    def t_recv(i):
        for k in range(4):
            t_copy(i, k // 2, k % 2, k).wait_recv()
        return jnp.concatenate([tdst[i, k].astype(f32) for k in range(4)], axis=1)

    lax.fori_loop(0, TOK // 32, norm, 0)
    gram(1, n_all, n_all)
    start(core_cp[1])
    g_cot.ring_fwd()
    core_done(1)
    for cp in w_x:
        cp.wait_recv()
    start(w_core)
    g_cot.middle(0)
    g_cot.middle(1)
    g_cot.own_half()
    g_cot.tail_fwd()
    x_done(1)
    g_cot.finish()
    w_core.wait_recv()

    acc[...] = jnp.zeros_like(acc)

    def og(b, _):
        w_blk = w_all[b // 2, pl.ds((b % 2) * 2, 2)].reshape(B, B)
        acc[...] += dot(cot_all[b], w_blk)
        return 0

    lax.fori_loop(0, 8, og, 0)
    for s in range(2):
        rows = pl.ds(s * ORBS, ORBS)
        og_s = (acc[rows, :] * keep_s[rows, :]).astype(bf16)
        for hd in range(2):
            v = dot_t(probs[s, hd], og_s[:, hd * 128:(hd + 1) * 128])
            v_all[f, rows, pl.ds(hd * 128, 128)] = v.astype(bf16)
    g_v.begin_z()
    g_v.begin_y()
    gram(0, n_all, v_all)
    start(core_cp[0])
    z_done(1)
    agz_start()
    core_done(0)
    g_v.ring_fwd()
    g_v.middle(0)
    x_done(0)
    g_v.own_half()
    ga.gram()
    g_v.middle(1)
    ga.core_done()
    agz_done()
    grad = z_done(0)
    t_core(0, grad)
    gx[f] = grad.astype(bf16)
    g_v.tail_fwd()
    t_send(0)
    ga.x_done()
    g_v.finish()
    gb.gram()
    ga.z_done()
    gb.core_done()
    x0 = t_recv(0)
    step_send(0, x0)
    agx_done()
    gb.x_done()
    agc_done()
    a_alpha = alpha_of(1)
    c1 = 4.0 * x0 - a_alpha * step_mul(0, 1)
    step_send(1, c1)
    gb.z_done()
    ga.agz_done()
    c2 = 6.0 * x0 - a_alpha * step_mul(1, 1)
    step_send(2, c2)
    gb.agz_done()
    for cp in gx_cp + [grad_part]:
        start(cp)
    ga.agx_done()
    c3 = 4.0 * x0 - a_alpha * step_mul(2, 1)
    t_core(1, c3)
    t_send(1)
    gb.agx_done()
    ga.agc_done()
    l0 = t_recv(1)
    step_send(3, l0)
    gb.agc_done()
    g_alpha = alpha_of(2)
    c1 = 4.0 * l0 - g_alpha * step_mul(3, 2)
    step_send(4, c1)
    for cp in gx_cp + [grad_part]:
        cp.wait_recv()
    grads = jnp.concatenate([grad2[0], grad2[1]], axis=1)
    q0 = both(2, lambda b: gx[b]) + damping * grads
    c2 = 6.0 * l0 - g_alpha * step_mul(4, 2)
    step_send(5, c2)

    fin[0] = total(4.0 * grads * l0 - g_alpha * (q0 * c2))
    fc = start(copy(fin.at[0], fin.at[1], at(dc=1)))
    fx = [copy(fin.at[2], fin.at[3 + i], at(dz=a, dx=b)) for i, (a, b) in enumerate(dp_offs)]
    fy = [copy(fin.at[18], fin.at[19 + i], at(dy=j)) for i, j in enumerate((2, 1, 3))]
    fc.wait_recv()
    fin[2] = fin[0] + fin[1]
    for cp in fx:
        start(cp)
    c3 = 4.0 * l0 - g_alpha * step_mul(5, 2)
    ab = a_alpha * g_alpha
    for cp in fx:
        cp.wait_recv()
    t = fin[2]
    for i in range(15):
        t = t + fin[3 + i]
    fin[18] = t
    for cp in fy:
        start(cp)
    tt[0:R, :] = c3 * ab
    for cp in fy:
        cp.wait_recv()
    for i in range(3):
        t = t + fin[19 + i]
    inner = t[0:1, 0:1] * ab
    out[...] = tt[0:R, pl.ds(pl.multiple_of(h * B, B), B)] * (float(D) / jnp.sqrt(inner + epsilon))

    for cp in started:
        cp.wait_send()
    for i in range(2):
        for e in range(2):
            for m in range(2):
                @pl.when(jnp.logical_not(t_here(i, e, m)))
                def _(i=i, e=e, m=m):
                    t_copy(i, e, m, 0).wait_send()
    assert count[0] <= NSEM


def per_device(occupations, stream, norm_gain, probs, w_out, cotangent):
    vm = pl.BlockSpec(memory_space=pltpu.VMEM)
    hb = pl.BlockSpec(memory_space=pl.ANY)
    V = pltpu.VMEM
    return pl.pallas_call(
        kernel,
        out_shape=jax.ShapeDtypeStruct((R, B), f32),
        in_specs=[vm, hb, vm, hb, hb, hb],
        out_specs=vm,
        scratch_shapes=[
            V((8, TOK, B), bf16),
            V((8, TOK, B), bf16),
            V((8, TOK, B), bf16),
            V((8, TOK, B), bf16),
            V((4, 4, 2, R, B), bf16),
            V((2, 2, ORBS, ORBS), bf16),
            V((TOK, B), f32),
            V((TOK, 1), f32),
            V((3, 16, 2, R, B), bf16),
            V((16, 2, R, B), f32),
            V((4, 4, R, B), f32),
            V((4, R, B), f32),
            V((3, 16, R, B), bf16),
            V((3, 4, 4, R, B), bf16),
            V((3, 3, 4, R, B), bf16),
            V((3, 4, R, B), bf16),
            V((3, 3, R, B), bf16),
            V((2, 2, 4, 4, 2, 2, R // 2, B), bf16),
            V((2, 4, R // 2, B), bf16),
            V((2, 3, R // 2, B), bf16),
            V((2, R, B), f32),
            V((8, R, B), bf16),
            V((2, 2, 2, R, 128), f32),
            V((2, 2, R, 128), f32),
            V((2, 2, 2, R, 128), bf16),
            V((2, 4, R, 128), bf16),
            V((R, 2 * B), f32),
            V((6, 4, 2, R, B), bf16),
            V((2, 4, 8, 128), f32),
            V((2, 14, 8, 128), f32),
            V((22, 8, 128), f32),
            pltpu.SemaphoreType.DMA((4,)),
            pltpu.SemaphoreType.DMA((NSEM,)),
            pltpu.SemaphoreType.DMA((NSEM,)),
        ],
        compiler_params=pltpu.CompilerParams(
            collective_id=0, has_side_effects=True, vmem_limit_bytes=56 << 20),
    )(occupations, stream, norm_gain.reshape(1, D), probs, w_out.T, cotangent)


def solution(mesh):
    placed = (
        P("dp", None),
        P("dp", "fac"),
        P(),
        P("dp", "fac", None, None),
        P("fac", "dp"),
        P("dp", "fac"),
    )
    return jax.shard_map(
        per_device, mesh=mesh, in_specs=placed, out_specs=P("dp", "fac"), check_vma=False
    )
```

```python
import jax
import jax.numpy as jnp
from jax import lax
from jax.experimental import pallas as pl
from jax.experimental.pallas import tpu as pltpu
from jax.sharding import PartitionSpec as P

ORBS = 256
NE = 48
TOK = 512
D = 2048
B = 256
R = 64
SCALE = 1.0 / 16384
damping = 0.1
epsilon = 1e-06
bf16 = jnp.bfloat16
f32 = jnp.float32
NSEM = 240


def dot(a, b):
    return lax.dot_general(a, b, (((1,), (0,)), ((), ())), preferred_element_type=f32)


def dot_t(a, b):
    return lax.dot_general(a, b, (((0,), (0,)), ((), ())), preferred_element_type=f32)


def kernel(occ, stream_h, gain, probs_h, w_h, cot_h, out,
           cot_all, st_all, n_all, v_all, w_all, probs, acc, keep_s,
           part, part_f, s1_f, s2_f, rc_b, s1_b, rx_b, s2_b, rz_b, slab, s2g, rzg,
           grad2, gx, tp, tpo, tsrc, tdst, tt, xg, nsrc, nbuf, fin, lsem, ssem, rsem):
    d = lax.axis_index("dp")
    f = lax.axis_index("fac")
    z, x, c = d // 8, (d // 2) % 4, d % 2
    h, y = f // 4, f % 4
    fd = d // 4
    mesh_id = pl.DeviceIdType.MESH

    def at(dh=0, dy=0, dz=0, dx=0, dc=0):
        nd = (((z + dz) % 4) * 4 + (x + dx) % 4) * 2 + (c + dc) % 2
        nf = ((h + dh) % 2) * 4 + (y + dy) % 4
        return {"dp": nd, "fac": nf}

    count = [0]
    started = []

    def copy(src, dst, dev):
        i = count[0]
        count[0] += 1
        return pltpu.make_async_remote_copy(
            src_ref=src, dst_ref=dst, send_sem=ssem.at[i], recv_sem=rsem.at[i],
            device_id=dev, device_id_type=pl.DeviceIdType.MESH)

    def start(cp):
        cp.start()
        started.append(cp)
        return cp

    fac_offs = [(1, 2), (1, 1), (1, 3), (1, 0), (0, 2), (0, 1), (0, 3)]
    dp_offs = [(a, b) for a in range(4) for b in range(4) if (a, b) != (0, 0)]
    z8_offs = [(1, 0), (1, 1), (1, 2), (1, 3), (0, 2), (0, 1), (0, 3)]

    bar = pltpu.get_barrier_semaphore()

    def greet(dev):
        pl.semaphore_signal(bar, inc=1, device_id=dev, device_id_type=mesh_id)

    for a, b in fac_offs:
        greet(at(dh=a, dy=b))
    for a, b in dp_offs:
        greet(at(dz=a, dx=b))
    greet(at(dc=1))
    for j in (1, 2, 3):
        greet(at(dh=1, dz=j))
        greet(at(dy=j, dc=1))
    own0 = fd == f
    own1 = fd % 4 == y
    pair = x % 2
    for e in range(2):
        for kk in range(2):
            src_d = 4 * (e * 4 + y) + 2 * kk + pair

            @pl.when(jnp.logical_not(own0 & (d == src_d)))
            def _(src_d=src_d):
                greet({"dp": src_d, "fac": fd})

            @pl.when(jnp.logical_not(own1 & (d == src_d)))
            def _(src_d=src_d):
                greet({"dp": src_d, "fac": h * 4 + fd % 4})

    local = [pltpu.make_async_copy(a, b, lsem.at[i]) for i, (a, b) in enumerate([
        (stream_h, st_all.at[f]), (cot_h, cot_all.at[f]), (w_h, w_all.at[z, x, c]), (probs_h, probs)])]
    for cp in local:
        cp.start()
    pl.semaphore_wait(bar, 7 + 15 + 1 + 3 + 3 + 8 - (own0 & (pair == c)).astype(jnp.int32) - (own1 & (pair == c)).astype(jnp.int32))

    class Gather:
        def __init__(self, buf):
            other = (1 - h) * 4 + y
            self.buf = buf
            self.first = [self.piece(f, k, dict(dh=1)) for k in range(2)]
            self.ring = [[self.piece(f, 0, dict(dy=1)), self.piece(f, 1, dict(dy=3))],
                         [self.piece(f, 1, dict(dy=1)), self.piece(f, 0, dict(dy=3))]]
            self.fwd = [[self.piece(other, k, dict(dy=1)), self.piece(other, k, dict(dy=3))] for k in range(2)]
            self.hop = [[self.piece(e * 4 + (y + 3) % 4, 0, dict(dy=1)), self.piece(e * 4 + (y + 1) % 4, 1, dict(dy=3))]
                        for e in (h, 1 - h)]

        def piece(self, block, k, to):
            ref = self.buf.at[block, pl.ds(k * 256, 256)]
            return copy(ref, ref, at(**to))

        def begin_z(self):
            for cp in self.first:
                start(cp)

        def begin_y(self):
            for cp in self.ring[0] + self.ring[1]:
                start(cp)

        def ring_fwd(self):
            for i in range(2):
                self.ring[0][i].wait_recv()
                start(self.hop[0][i])

        def middle(self, k):
            self.first[k].wait_recv()
            for cp in self.fwd[k]:
                start(cp)

        def tail_fwd(self):
            self.fwd[0][0].wait_recv()
            start(self.hop[1][0])
            self.fwd[1][1].wait_recv()
            start(self.hop[1][1])

        def own_half(self):
            for cp in self.ring[1] + self.hop[0]:
                cp.wait_recv()

        def finish(self):
            for cp in [self.fwd[0][1], self.fwd[1][0]] + self.hop[1]:
                cp.wait_recv()

    g_st, g_cot, g_v = Gather(st_all), Gather(cot_all), Gather(v_all)
    local[0].wait()
    g_st.begin_z()
    g_st.begin_y()
    row = lax.broadcasted_iota(jnp.int32, (ORBS, ORBS), 0)
    col = lax.broadcasted_iota(jnp.int32, (ORBS, ORBS), 1)
    pos = lax.broadcasted_iota(jnp.int32, (ORBS, 1), 0).astype(f32)
    for s in range(2):
        ones = occ[pl.ds(s, 1), :].astype(f32)
        before = jnp.sum(jnp.where(col < row, ones, 0.0), axis=1, keepdims=True)
        forced = (before == float(NE)) | (pos - before == float(ORBS - NE))
        keep_s[pl.ds(s * ORBS, ORBS), :] = jnp.where(forced, 0.0, 1.0)
    for cp in local[1:]:
        cp.wait()
    w_z = [copy(w_all.at[z, x, c], w_all.at[z, x, c], at(dz=j)) for j in (2, 1, 3)]
    w_x = [copy(w_all.at[:, x, c], w_all.at[:, x, c], at(dx=j)) for j in (1, 3, 2)]
    w_core = copy(w_all.at[:, :, c], w_all.at[:, :, c], at(dc=1))
    for cp in w_z:
        start(cp)
    g_st.ring_fwd()
    g_st.middle(0)
    g_st.middle(1)
    g_cot.begin_z()
    for cp in w_z:
        cp.wait_recv()
    for cp in w_x:
        start(cp)
    g_st.tail_fwd()
    g_cot.begin_y()
    g_st.own_half()
    g_st.finish()

    def norm(t, _):
        rows = pl.ds(pl.multiple_of(t * 32, 32), 32)
        sq = jnp.zeros((32, B), f32)
        for b in range(8):
            v = st_all[b, rows, :].astype(f32)
            sq = sq + v * v
        inv = lax.rsqrt(jnp.sum(sq, axis=1, keepdims=True) * (1.0 / D) + epsilon)
        for b in range(8):
            v = st_all[b, rows, :].astype(f32)
            n_all[b, rows, :] = (v * inv * gain[:, b * B:(b + 1) * B]).astype(bf16)
        return 0

    def gram(k, left, right):
        def body(b, _):
            p = dot_t(left[b], right[f]) * SCALE
            part[k, pl.ds(b * 2, 2)] = p.astype(bf16).reshape(2, 2, R, B)
            if k == 0:
                part_f[pl.ds(b * 2, 2)] = p.reshape(2, 2, R, B)
            return 0
        lax.fori_loop(0, 8, body, 0)

    core_cp = [copy(part.at[k, :, 1 - c], rc_b.at[k], at(dc=1)) for k in range(2)]
    x_cp = [[copy(s1_b.at[k, :, (x + j) % 4], rx_b.at[k, j - 1], at(dx=j)) for j in (1, 3, 2)] for k in range(2)]

    def core_done(k):
        core_cp[k].wait_recv()

        def body(q, _):
            mine = part_f[pl.ds(q * 4, 4), c] if k == 0 else part[k, pl.ds(q * 4, 4), c].astype(f32)
            t = mine + rc_b[k, pl.ds(q * 4, 4)].astype(f32)
            s1_b[k, q] = t.astype(bf16)
            if k == 0:
                s1_f[q] = t
            return 0
        lax.fori_loop(0, 4, body, 0)
        for cp in x_cp[k]:
            start(cp)

    z_cp = [[copy(s2_b.at[k, (z + j) % 4], rz_b.at[k, j - 1], at(dz=j)) for j in (2, 1, 3)] for k in range(2)]

    def x_done(k):
        for cp in x_cp[k]:
            cp.wait_recv()
        t = s1_f[:, x] if k == 0 else s1_b[k, :, x].astype(f32)
        for j in range(3):
            t = t + rx_b[k, j].astype(f32)
        s2_b[k] = t.astype(bf16)
        if k == 0:
            s2_f[...] = t
        for cp in z_cp[k]:
            start(cp)

    agz_cp = [copy(slab.at[0, h, z, x, c], slab.at[0, h, z, x, c], at(dh=a, dz=b)) for a, b in z8_offs]
    agx_cp = [copy(slab.at[0, :, :, x, c], slab.at[0, :, :, x, c], at(dx=j)) for j in (1, 3, 2)]
    agc_cp = copy(slab.at[0, :, :, :, c], slab.at[0, :, :, :, c], at(dc=1))
    nz_cp = [[copy(nsrc.at[k, 0], nbuf.at[k, i], at(dh=a, dz=b)) for i, (a, b) in enumerate(z8_offs)] for k in range(2)]
    nx_cp = [[copy(nsrc.at[k, 1], nbuf.at[k, 7 + i], at(dx=j)) for i, j in enumerate((1, 3, 2))] for k in range(2)]
    nc_cp = [[copy(nsrc.at[k, 2], nbuf.at[k, 10], at(dc=1))] for k in range(2)]
    ny_cp = [[copy(nsrc.at[k, 3], nbuf.at[k, 11 + i], at(dy=j)) for i, j in enumerate((1, 3, 2))] for k in range(2)]

    def total(v):
        return jnp.broadcast_to(
            jnp.sum(jnp.sum(v, axis=0, keepdims=True), axis=1, keepdims=True), (8, 128))

    def gathered(k, cps, nst, first, n):
        for cp in cps:
            cp.wait_recv()
        t = nsrc[k, nst]
        for i in range(n):
            t = t + nbuf[k, first + i]
        nsrc[k, nst + 1] = t

    grad_part = copy(grad2.at[h], grad2.at[h], at(dh=1))
    gx_cp = [copy(gx.at[f], gx.at[f], at(dh=a, dy=b)) for a, b in fac_offs]

    def z_done(k):
        for cp in z_cp[k]:
            cp.wait_recv()
        t = s2_f[z] if k == 0 else s2_b[k, z].astype(f32)
        for j in range(3):
            t = t + rz_b[k, j].astype(f32)
        if k == 0:
            grad2[h] = t
            return t
        slab[0, h, z, x, c] = t.astype(bf16).reshape(2, R // 2, B)
        ri = d * R + lax.broadcasted_iota(jnp.int32, (R, B), 0)
        ci = f * B + lax.broadcasted_iota(jnp.int32, (R, B), 1)
        t = t + jnp.where(ri == ci, damping, 0.0)
        nsrc[k - 1, 0] = total(t * t)
        return None

    def agz_start():
        for cp in agz_cp + nz_cp[0]:
            start(cp)

    def agz_done():
        gathered(0, agz_cp + nz_cp[0], 0, 0, 7)
        for cp in agx_cp + nx_cp[0]:
            start(cp)

    def agx_done():
        gathered(0, agx_cp + nx_cp[0], 1, 7, 3)
        for cp in [agc_cp] + nc_cp[0]:
            start(cp)

    def agc_done():
        gathered(0, [agc_cp] + nc_cp[0], 2, 10, 1)
        for cp in ny_cp[0]:
            start(cp)

    class Half:
        def __init__(self, q):
            self.q = q
            hh = h if q == 0 else 1 - h
            self.hh = hh
            self.planes = pl.ds(2 * hh, 2)
            rows = pl.ds(8 * hh, 8)
            self.core = copy(part.at[2, rows, 1 - c], rc_b.at[2, rows], at(dc=1))
            self.xs = [copy(s1_b.at[2, self.planes, (x + j) % 4], rx_b.at[2, j - 1, self.planes], at(dx=j)) for j in (1, 3, 2)]
            self.zs = [copy(s2g.at[q, (z + j) % 4], rzg.at[q, j - 1], at(dz=j)) for j in (2, 1, 3)]
            own_piece = slab.at[1, h, 2 * hh + z // 2, x, c, z % 2]
            self.agz = [copy(own_piece, own_piece, at(dh=a, dz=b)) for a, b in z8_offs]
            regions = [(e, 2 * e if q == 0 else 2 * (1 - e)) for e in range(2)]
            self.agx = [copy(slab.at[1, e, r:r + 2, x, c], slab.at[1, e, r:r + 2, x, c], at(dx=j))
                        for j in (1, 3, 2) for e, r in regions]
            self.agc = [copy(slab.at[1, e, r:r + 2, :, c], slab.at[1, e, r:r + 2, :, c], at(dc=1)) for e, r in regions]

        def gram(self):
            def body(i, _):
                b = self.hh * 4 + i
                p = dot_t(v_all[b], v_all[f]) * SCALE
                part[2, pl.ds(b * 2, 2)] = p.astype(bf16).reshape(2, 2, R, B)
                return 0
            lax.fori_loop(0, 4, body, 0)
            start(self.core)

        def core_done(self):
            self.core.wait_recv()

            def body(i, _):
                q = 2 * self.hh + i
                s1_b[2, q] = (part[2, pl.ds(q * 4, 4), c].astype(f32)
                              + rc_b[2, pl.ds(q * 4, 4)].astype(f32)).astype(bf16)
                return 0
            lax.fori_loop(0, 2, body, 0)
            for cp in self.xs:
                start(cp)

        def x_done(self):
            for cp in self.xs:
                cp.wait_recv()
            t = s1_b[2, self.planes, x].astype(f32)
            for j in range(3):
                t = t + rx_b[2, j, self.planes].astype(f32)
            s2g[self.q] = t.astype(bf16).reshape(4, R // 2, B)
            for cp in self.zs:
                start(cp)

        def z_done(self):
            for cp in self.zs:
                cp.wait_recv()
            t = s2g[self.q, z].astype(f32)
            for j in range(3):
                t = t + rzg[self.q, j].astype(f32)
            slab[1, h, 2 * self.hh + z // 2, x, c, z % 2] = t.astype(bf16)
            first = ((2 * self.hh + z // 2) * 8 + x * 2 + c) * R + (z % 2) * (R // 2)
            ri = first + lax.broadcasted_iota(jnp.int32, (R // 2, B), 0)
            ci = f * B + lax.broadcasted_iota(jnp.int32, (R // 2, B), 1)
            t = t + jnp.where(ri == ci, damping, 0.0)
            if self.q == 0:
                nsrc[1, 0] = total(t * t)
            else:
                nsrc[1, 0] += total(t * t)
            for cp in self.agz + (nz_cp[1] if self.q else []):
                start(cp)

        def agz_done(self):
            if self.q:
                gathered(1, self.agz + nz_cp[1], 0, 0, 7)
            else:
                for cp in self.agz:
                    cp.wait_recv()
            for cp in self.agx + (nx_cp[1] if self.q else []):
                start(cp)

        def agx_done(self):
            if self.q:
                gathered(1, self.agx + nx_cp[1], 1, 7, 3)
            else:
                for cp in self.agx:
                    cp.wait_recv()
            for cp in self.agc + (nc_cp[1] if self.q else []):
                start(cp)

        def agc_done(self):
            if self.q:
                gathered(1, self.agc + nc_cp[1], 2, 10, 1)
                for cp in ny_cp[1]:
                    start(cp)
            else:
                for cp in self.agc:
                    cp.wait_recv()

    ga, gb = Half(0), Half(1)

    def alpha_of(k):
        for cp in ny_cp[k - 1]:
            cp.wait_recv()
        t = nsrc[k - 1, 3]
        for i in range(3):
            t = t + nbuf[k - 1, 11 + i]
        return (1.0 / jnp.sqrt(t))[0:1, 0:1]

    def slab_rows(k, e, b):
        return slab[k - 1, e, b // 2, (b % 2) * 2:(b % 2) * 2 + 2].reshape(B, B)

    def both(k, block):
        cols = []
        for e in range(2):
            t = dot(block(0), slab_rows(k, e, 0))
            for b in range(1, 8):
                t = t + dot(block(b), slab_rows(k, e, b))
            cols.append(t)
        return jnp.concatenate(cols, axis=1)

    x_own = [None] * 6
    step_cp = [[copy(xg.at[i, y], xg.at[i, y], at(dy=j)) for j in (2, 1, 3)] for i in range(6)]

    def step_send(i, value):
        v = value.astype(bf16)
        xg[i, y, 0] = v[:, :B]
        xg[i, y, 1] = v[:, B:]
        x_own[i] = value
        for cp in step_cp[i]:
            start(cp)

    def step_mul(i, k):
        for cp in step_cp[i]:
            cp.wait_recv()
        return x_own[i] * damping + both(k, lambda b: xg[i, b % 4, b // 4])

    t_base = []
    for _ in range(2):
        t_base.append(count[0])
        count[0] += 4
    t_slot = (fd // 4) * 2 + pair
    t_pair = [copy(tpo.at[0, 0], tp.at[0, 0, c], at(dc=1)),
              copy(tpo.at[1], tp.at[1, :, c], at(dc=1))]

    def t_copy(i, e, m, slot):
        if i == 0:
            dev = {"dp": 4 * f + 2 * c + m, "fac": e * 4 + fd % 4}
        else:
            dev = {"dp": 4 * (e * 4 + y) + 2 * c + m, "fac": h * 4 + fd % 4}
        return pltpu.make_async_remote_copy(
            src_ref=tsrc.at[i, 0 if i == 0 else e, m], dst_ref=tdst.at[i, slot],
            send_sem=ssem.at[t_base[i] + e * 2 + m], recv_sem=rsem.at[t_base[i] + slot],
            device_id=dev, device_id_type=pl.DeviceIdType.MESH)

    def t_here(i, e, m):
        if i == 0:
            return own0 & (d == 4 * f + 2 * c + m) & (h == e)
        return own1 & (d == 4 * (e * 4 + y) + 2 * c + m)

    def t_core(i, value):
        for e in range(i + 1):
            lo = value[:, e * B:e * B + 128]
            hi = value[:, e * B + 128:(e + 1) * B]
            tp[i, e, c] = jnp.where(c == 0, lo, hi).astype(bf16)
            tpo[i, e] = jnp.where(c == 0, hi, lo).astype(bf16)
        start(t_pair[i])

    def t_send(i):
        t_pair[i].wait_recv()
        for e in range(i + 1):
            tsrc[i, e] = tp[i, e].astype(f32).reshape(128, 128).T.astype(bf16).reshape(2, R, 128)
        for e in range(2):
            for m in range(2):
                here = t_here(i, e, m)

                @pl.when(here)
                def _(e=e, m=m):
                    pltpu.make_async_copy(
                        tsrc.at[i, 0 if i == 0 else e, m], tdst.at[i, t_slot],
                        rsem.at[t_base[i] + t_slot]).start()

                @pl.when(jnp.logical_not(here))
                def _(e=e, m=m):
                    t_copy(i, e, m, t_slot).start()

    def t_recv(i):
        for k in range(4):
            t_copy(i, k // 2, k % 2, k).wait_recv()
        return jnp.concatenate([tdst[i, k].astype(f32) for k in range(4)], axis=1)

    lax.fori_loop(0, TOK // 32, norm, 0)
    gram(1, n_all, n_all)
    start(core_cp[1])
    g_cot.ring_fwd()
    core_done(1)
    for cp in w_x:
        cp.wait_recv()
    start(w_core)
    g_cot.middle(0)
    g_cot.middle(1)
    g_cot.own_half()
    g_cot.tail_fwd()
    x_done(1)
    g_cot.finish()
    w_core.wait_recv()

    acc[...] = jnp.zeros_like(acc)

    def og(b, _):
        w_blk = w_all[b // 2, pl.ds((b % 2) * 2, 2)].reshape(B, B)
        acc[...] += dot(cot_all[b], w_blk)
        return 0

    lax.fori_loop(0, 8, og, 0)
    for s in range(2):
        rows = pl.ds(s * ORBS, ORBS)
        og_s = (acc[rows, :] * keep_s[rows, :]).astype(bf16)
        for hd in range(2):
            v = dot_t(probs[s, hd], og_s[:, hd * 128:(hd + 1) * 128])
            v_all[f, rows, pl.ds(hd * 128, 128)] = v.astype(bf16)
    g_v.begin_z()
    g_v.begin_y()
    gram(0, n_all, v_all)
    start(core_cp[0])
    z_done(1)
    agz_start()
    core_done(0)
    g_v.ring_fwd()
    g_v.middle(0)
    x_done(0)
    g_v.own_half()
    ga.gram()
    g_v.middle(1)
    ga.core_done()
    agz_done()
    grad = z_done(0)
    t_core(0, grad)
    gx[f] = grad.astype(bf16)
    g_v.tail_fwd()
    t_send(0)
    ga.x_done()
    g_v.finish()
    gb.gram()
    ga.z_done()
    gb.core_done()
    x0 = t_recv(0)
    step_send(0, x0)
    agx_done()
    gb.x_done()
    agc_done()
    a_alpha = alpha_of(1)
    c1 = 4.0 * x0 - a_alpha * step_mul(0, 1)
    step_send(1, c1)
    gb.z_done()
    ga.agz_done()
    c2 = 6.0 * x0 - a_alpha * step_mul(1, 1)
    step_send(2, c2)
    gb.agz_done()
    for cp in gx_cp + [grad_part]:
        start(cp)
    ga.agx_done()
    c3 = 4.0 * x0 - a_alpha * step_mul(2, 1)
    t_core(1, c3)
    t_send(1)
    gb.agx_done()
    ga.agc_done()
    l0 = t_recv(1)
    step_send(3, l0)
    gb.agc_done()
    g_alpha = alpha_of(2)
    c1 = 4.0 * l0 - g_alpha * step_mul(3, 2)
    step_send(4, c1)
    for cp in gx_cp + [grad_part]:
        cp.wait_recv()
    grads = jnp.concatenate([grad2[0], grad2[1]], axis=1)
    q0 = both(2, lambda b: gx[b]) + damping * grads
    c2 = 6.0 * l0 - g_alpha * step_mul(4, 2)
    fin[0] = total(4.0 * grads * l0 - g_alpha * (q0 * c2))
    yc_offs = [(2, 0), (2, 1), (1, 0), (3, 0), (1, 1), (3, 1), (0, 1)]
    fa = [copy(fin.at[0], fin.at[1 + i], at(dy=a, dc=b)) for i, (a, b) in enumerate(yc_offs)]
    fx = [copy(fin.at[8], fin.at[9 + i], at(dz=a, dx=b)) for i, (a, b) in enumerate(dp_offs)]
    for cp in fa:
        start(cp)
    step_send(5, c2)
    for cp in fa:
        cp.wait_recv()
    t = fin[0]
    for i in range(7):
        t = t + fin[1 + i]
    fin[8] = t
    for cp in fx:
        start(cp)
    c3 = 4.0 * l0 - g_alpha * step_mul(5, 2)
    ab = a_alpha * g_alpha
    tt[0:R, :] = c3 * ab
    for cp in fx:
        cp.wait_recv()
    for i in range(15):
        t = t + fin[9 + i]
    inner = t[0:1, 0:1] * ab
    out[...] = tt[0:R, pl.ds(pl.multiple_of(h * B, B), B)] * (float(D) / jnp.sqrt(inner + epsilon))

    for cp in started:
        cp.wait_send()
    for i in range(2):
        for e in range(2):
            for m in range(2):
                @pl.when(jnp.logical_not(t_here(i, e, m)))
                def _(i=i, e=e, m=m):
                    t_copy(i, e, m, 0).wait_send()
    assert count[0] <= NSEM


def per_device(occupations, stream, norm_gain, probs, w_out, cotangent):
    vm = pl.BlockSpec(memory_space=pltpu.VMEM)
    hb = pl.BlockSpec(memory_space=pl.ANY)
    V = pltpu.VMEM
    return pl.pallas_call(
        kernel,
        out_shape=jax.ShapeDtypeStruct((R, B), f32),
        in_specs=[vm, hb, vm, hb, hb, hb],
        out_specs=vm,
        scratch_shapes=[
            V((8, TOK, B), bf16),
            V((8, TOK, B), bf16),
            V((8, TOK, B), bf16),
            V((8, TOK, B), bf16),
            V((4, 4, 2, R, B), bf16),
            V((2, 2, ORBS, ORBS), bf16),
            V((TOK, B), f32),
            V((TOK, 1), f32),
            V((3, 16, 2, R, B), bf16),
            V((16, 2, R, B), f32),
            V((4, 4, R, B), f32),
            V((4, R, B), f32),
            V((3, 16, R, B), bf16),
            V((3, 4, 4, R, B), bf16),
            V((3, 3, 4, R, B), bf16),
            V((3, 4, R, B), bf16),
            V((3, 3, R, B), bf16),
            V((2, 2, 4, 4, 2, 2, R // 2, B), bf16),
            V((2, 4, R // 2, B), bf16),
            V((2, 3, R // 2, B), bf16),
            V((2, R, B), f32),
            V((8, R, B), bf16),
            V((2, 2, 2, R, 128), bf16),
            V((2, 2, R, 128), bf16),
            V((2, 2, 2, R, 128), bf16),
            V((2, 4, R, 128), bf16),
            V((R, 2 * B), f32),
            V((6, 4, 2, R, B), bf16),
            V((2, 4, 8, 128), f32),
            V((2, 14, 8, 128), f32),
            V((24, 8, 128), f32),
            pltpu.SemaphoreType.DMA((4,)),
            pltpu.SemaphoreType.DMA((NSEM,)),
            pltpu.SemaphoreType.DMA((NSEM,)),
        ],
        compiler_params=pltpu.CompilerParams(
            collective_id=0, has_side_effects=True, vmem_limit_bytes=56 << 20),
    )(occupations, stream, norm_gain.reshape(1, D), probs, w_out.T, cotangent)


def solution(mesh):
    placed = (
        P("dp", None),
        P("dp", "fac"),
        P(),
        P("dp", "fac", None, None),
        P("fac", "dp"),
        P("dp", "fac"),
    )
    return jax.shard_map(
        per_device, mesh=mesh, in_specs=placed, out_specs=P("dp", "fac"), check_vma=False
    )
```

```python
import jax
import jax.numpy as jnp
from jax import lax
from jax.experimental import pallas as pl
from jax.experimental.pallas import tpu as pltpu
from jax.sharding import PartitionSpec as P

ORBS = 256
NE = 48
TOK = 512
D = 2048
B = 256
R = 64
SCALE = 1.0 / 16384
damping = 0.1
epsilon = 1e-06
bf16 = jnp.bfloat16
f32 = jnp.float32
NSEM = 280


def dot(a, b):
    return lax.dot_general(a, b, (((1,), (0,)), ((), ())), preferred_element_type=f32)


def dot_t(a, b):
    return lax.dot_general(a, b, (((0,), (0,)), ((), ())), preferred_element_type=f32)


def kernel(occ, stream_h, gain, probs_h, w_h, cot_h, out,
           cot_all, st_all, n_all, v_all, w_all, probs, acc, keep_s,
           part, part_f, s1_f, s2_f, rc_b, s1_b, rx_b, s2_b, rz_b, slab, s2g, rzg,
           grad2, gx, tp, tpo, tsrc, tdst, tt, xg, nsrc, nbuf, fin, lsem, ssem, rsem):
    d = lax.axis_index("dp")
    f = lax.axis_index("fac")
    z, x, c = d // 8, (d // 2) % 4, d % 2
    h, y = f // 4, f % 4
    fd = d // 4
    mesh_id = pl.DeviceIdType.MESH

    def at(dh=0, dy=0, dz=0, dx=0, dc=0):
        nd = (((z + dz) % 4) * 4 + (x + dx) % 4) * 2 + (c + dc) % 2
        nf = ((h + dh) % 2) * 4 + (y + dy) % 4
        return {"dp": nd, "fac": nf}

    count = [0]
    started = []

    def copy(src, dst, dev):
        i = count[0]
        count[0] += 1
        return pltpu.make_async_remote_copy(
            src_ref=src, dst_ref=dst, send_sem=ssem.at[i], recv_sem=rsem.at[i],
            device_id=dev, device_id_type=pl.DeviceIdType.MESH)

    def start(cp):
        cp.start()
        started.append(cp)
        return cp

    fac_offs = [(1, 2), (1, 1), (1, 3), (1, 0), (0, 2), (0, 1), (0, 3)]
    dp_offs = [(a, b) for a in range(4) for b in range(4) if (a, b) != (0, 0)]
    z8_offs = [(1, 0), (1, 1), (1, 2), (1, 3), (0, 2), (0, 1), (0, 3)]

    bar = pltpu.get_barrier_semaphore()

    def greet(dev):
        pl.semaphore_signal(bar, inc=1, device_id=dev, device_id_type=mesh_id)

    for a, b in fac_offs:
        greet(at(dh=a, dy=b))
    for a, b in dp_offs:
        greet(at(dz=a, dx=b))
    greet(at(dc=1))
    for j in (1, 2, 3):
        greet(at(dh=1, dz=j))
        greet(at(dy=j, dc=1))
    own0 = fd == f
    own1 = fd % 4 == y
    pair = x % 2
    for e in range(2):
        for kk in range(2):
            src_d = 4 * (e * 4 + y) + 2 * kk + pair

            @pl.when(jnp.logical_not(own0 & (d == src_d)))
            def _(src_d=src_d):
                greet({"dp": src_d, "fac": fd})

            @pl.when(jnp.logical_not(own1 & (d == src_d)))
            def _(src_d=src_d):
                greet({"dp": src_d, "fac": h * 4 + fd % 4})

    local = [pltpu.make_async_copy(a, b, lsem.at[i]) for i, (a, b) in enumerate([
        (stream_h, st_all.at[f]), (cot_h, cot_all.at[f]), (w_h, w_all.at[z, x, c]), (probs_h, probs)])]
    for cp in local:
        cp.start()
    pl.semaphore_wait(bar, 7 + 15 + 1 + 3 + 3 + 8 - (own0 & (pair == c)).astype(jnp.int32) - (own1 & (pair == c)).astype(jnp.int32))

    class Gather:
        def __init__(self, buf):
            other = (1 - h) * 4 + y
            self.buf = buf
            self.first = [self.piece(f, k, dict(dh=1), 128) for k in range(4)]
            self.ring = [[self.piece(f, 0, dict(dy=1)), self.piece(f, 1, dict(dy=3))],
                         [self.piece(f, 1, dict(dy=1)), self.piece(f, 0, dict(dy=3))]]
            self.fwd = [[self.piece(other, k, dict(dy=1), 128), self.piece(other, k, dict(dy=3), 128)] for k in range(4)]
            up, down = (y + 3) % 4, (y + 1) % 4
            self.hop = [self.piece(h * 4 + up, 0, dict(dy=1)), self.piece(h * 4 + down, 1, dict(dy=3))]
            self.far = [self.piece((1 - h) * 4 + (up if k < 2 else down), k, dict(dy=1 if k < 2 else 3), 128) for k in range(4)]

        def piece(self, block, k, to, n=256):
            ref = self.buf.at[block, pl.ds(k * n, n)]
            return copy(ref, ref, at(**to))

        def begin_z(self):
            for cp in self.first:
                start(cp)

        def begin_y(self):
            for cp in self.ring[0] + self.ring[1]:
                start(cp)

        def ring_fwd(self):
            for i in range(2):
                self.ring[0][i].wait_recv()
                start(self.hop[i])

        def middle(self, half):
            for k in (2 * half, 2 * half + 1):
                self.first[k].wait_recv()
                for cp in self.fwd[k]:
                    start(cp)

        def tail_fwd(self):
            for k in range(4):
                self.fwd[k][k // 2].wait_recv()
                start(self.far[k])

        def own_half(self):
            for cp in self.ring[1] + self.hop:
                cp.wait_recv()

        def finish(self):
            for k in range(4):
                self.fwd[k][1 - k // 2].wait_recv()
            for cp in self.far:
                cp.wait_recv()

    g_st, g_cot, g_v = Gather(st_all), Gather(cot_all), Gather(v_all)
    local[0].wait()
    g_st.begin_z()
    g_st.begin_y()
    row = lax.broadcasted_iota(jnp.int32, (ORBS, ORBS), 0)
    col = lax.broadcasted_iota(jnp.int32, (ORBS, ORBS), 1)
    pos = lax.broadcasted_iota(jnp.int32, (ORBS, 1), 0).astype(f32)
    for s in range(2):
        ones = occ[pl.ds(s, 1), :].astype(f32)
        before = jnp.sum(jnp.where(col < row, ones, 0.0), axis=1, keepdims=True)
        forced = (before == float(NE)) | (pos - before == float(ORBS - NE))
        keep_s[pl.ds(s * ORBS, ORBS), :] = jnp.where(forced, 0.0, 1.0)
    for cp in local[1:]:
        cp.wait()
    w_z = [copy(w_all.at[z, x, c], w_all.at[z, x, c], at(dz=j)) for j in (2, 1, 3)]
    w_x = [copy(w_all.at[:, x, c], w_all.at[:, x, c], at(dx=j)) for j in (1, 3, 2)]
    w_core = copy(w_all.at[:, :, c], w_all.at[:, :, c], at(dc=1))
    for cp in w_z:
        start(cp)
    g_st.ring_fwd()
    g_st.middle(0)
    g_st.middle(1)
    g_cot.begin_z()
    for cp in w_z:
        cp.wait_recv()
    for cp in w_x:
        start(cp)
    g_st.tail_fwd()
    g_cot.begin_y()
    g_st.own_half()
    g_st.finish()

    def norm(t, _):
        rows = pl.ds(pl.multiple_of(t * 32, 32), 32)
        sq = jnp.zeros((32, B), f32)
        for b in range(8):
            v = st_all[b, rows, :].astype(f32)
            sq = sq + v * v
        inv = lax.rsqrt(jnp.sum(sq, axis=1, keepdims=True) * (1.0 / D) + epsilon)
        for b in range(8):
            v = st_all[b, rows, :].astype(f32)
            n_all[b, rows, :] = (v * inv * gain[:, b * B:(b + 1) * B]).astype(bf16)
        return 0

    def gram(k, left, right):
        def body(b, _):
            p = dot_t(left[b], right[f]) * SCALE
            part[k, pl.ds(b * 2, 2)] = p.astype(bf16).reshape(2, 2, R, B)
            if k == 0:
                part_f[pl.ds(b * 2, 2)] = p.reshape(2, 2, R, B)
            return 0
        lax.fori_loop(0, 8, body, 0)

    core_cp = [copy(part.at[k, :, 1 - c], rc_b.at[k], at(dc=1)) for k in range(2)]
    x_cp = [[copy(s1_b.at[k, :, (x + j) % 4], rx_b.at[k, j - 1], at(dx=j)) for j in (1, 3, 2)] for k in range(2)]

    def core_done(k):
        core_cp[k].wait_recv()

        def body(q, _):
            mine = part_f[pl.ds(q * 4, 4), c] if k == 0 else part[k, pl.ds(q * 4, 4), c].astype(f32)
            t = mine + rc_b[k, pl.ds(q * 4, 4)].astype(f32)
            s1_b[k, q] = t.astype(bf16)
            if k == 0:
                s1_f[q] = t
            return 0
        lax.fori_loop(0, 4, body, 0)
        for cp in x_cp[k]:
            start(cp)

    z_cp = [[copy(s2_b.at[k, (z + j) % 4], rz_b.at[k, j - 1], at(dz=j)) for j in (2, 1, 3)] for k in range(2)]

    def x_done(k):
        for cp in x_cp[k]:
            cp.wait_recv()
        t = s1_f[:, x] if k == 0 else s1_b[k, :, x].astype(f32)
        for j in range(3):
            t = t + rx_b[k, j].astype(f32)
        s2_b[k] = t.astype(bf16)
        if k == 0:
            s2_f[...] = t
        for cp in z_cp[k]:
            start(cp)

    agz_cp = [copy(slab.at[0, h, z, x, c], slab.at[0, h, z, x, c], at(dh=a, dz=b)) for a, b in z8_offs]
    agx_cp = [copy(slab.at[0, :, :, x, c], slab.at[0, :, :, x, c], at(dx=j)) for j in (1, 3, 2)]
    agc_cp = copy(slab.at[0, :, :, :, c], slab.at[0, :, :, :, c], at(dc=1))
    nz_cp = [[copy(nsrc.at[k, 0], nbuf.at[k, i], at(dh=a, dz=b)) for i, (a, b) in enumerate(z8_offs)] for k in range(2)]
    nx_cp = [[copy(nsrc.at[k, 1], nbuf.at[k, 7 + i], at(dx=j)) for i, j in enumerate((1, 3, 2))] for k in range(2)]
    nc_cp = [[copy(nsrc.at[k, 2], nbuf.at[k, 10], at(dc=1))] for k in range(2)]
    ny_cp = [[copy(nsrc.at[k, 3], nbuf.at[k, 11 + i], at(dy=j)) for i, j in enumerate((1, 3, 2))] for k in range(2)]

    def total(v):
        return jnp.broadcast_to(
            jnp.sum(jnp.sum(v, axis=0, keepdims=True), axis=1, keepdims=True), (8, 128))

    def gathered(k, cps, nst, first, n):
        for cp in cps:
            cp.wait_recv()
        t = nsrc[k, nst]
        for i in range(n):
            t = t + nbuf[k, first + i]
        nsrc[k, nst + 1] = t

    grad_part = copy(grad2.at[h], grad2.at[h], at(dh=1))
    gx_cp = [copy(gx.at[f], gx.at[f], at(dh=a, dy=b)) for a, b in fac_offs]

    def z_done(k):
        for cp in z_cp[k]:
            cp.wait_recv()
        t = s2_f[z] if k == 0 else s2_b[k, z].astype(f32)
        for j in range(3):
            t = t + rz_b[k, j].astype(f32)
        if k == 0:
            grad2[h] = t
            return t
        slab[0, h, z, x, c] = t.astype(bf16).reshape(2, R // 2, B)
        ri = d * R + lax.broadcasted_iota(jnp.int32, (R, B), 0)
        ci = f * B + lax.broadcasted_iota(jnp.int32, (R, B), 1)
        t = t + jnp.where(ri == ci, damping, 0.0)
        nsrc[k - 1, 0] = total(t * t)
        return None

    def agz_start():
        for cp in agz_cp + nz_cp[0]:
            start(cp)

    def agz_done():
        gathered(0, agz_cp + nz_cp[0], 0, 0, 7)
        for cp in agx_cp + nx_cp[0]:
            start(cp)

    def agx_done():
        gathered(0, agx_cp + nx_cp[0], 1, 7, 3)
        for cp in [agc_cp] + nc_cp[0]:
            start(cp)

    def agc_done():
        gathered(0, [agc_cp] + nc_cp[0], 2, 10, 1)
        for cp in ny_cp[0]:
            start(cp)

    class Half:
        def __init__(self, q):
            self.q = q
            hh = h if q == 0 else 1 - h
            self.hh = hh
            self.planes = pl.ds(2 * hh, 2)
            rows = pl.ds(8 * hh, 8)
            self.core = copy(part.at[2, rows, 1 - c], rc_b.at[2, rows], at(dc=1))
            self.xs = [copy(s1_b.at[2, self.planes, (x + j) % 4], rx_b.at[2, j - 1, self.planes], at(dx=j)) for j in (1, 3, 2)]
            self.zs = [copy(s2g.at[q, (z + j) % 4], rzg.at[q, j - 1], at(dz=j)) for j in (2, 1, 3)]
            own_piece = slab.at[1, h, 2 * hh + z // 2, x, c, z % 2]
            self.agz = [copy(own_piece, own_piece, at(dh=a, dz=b)) for a, b in z8_offs]
            regions = [(e, 2 * e if q == 0 else 2 * (1 - e)) for e in range(2)]
            self.agx = [copy(slab.at[1, e, r:r + 2, x, c], slab.at[1, e, r:r + 2, x, c], at(dx=j))
                        for j in (1, 3, 2) for e, r in regions]
            self.agc = [copy(slab.at[1, e, r:r + 2, :, c], slab.at[1, e, r:r + 2, :, c], at(dc=1)) for e, r in regions]

        def gram(self):
            def body(i, _):
                b = self.hh * 4 + i
                p = dot_t(v_all[b], v_all[f]) * SCALE
                part[2, pl.ds(b * 2, 2)] = p.astype(bf16).reshape(2, 2, R, B)
                return 0
            lax.fori_loop(0, 4, body, 0)
            start(self.core)

        def core_done(self):
            self.core.wait_recv()

            def body(i, _):
                q = 2 * self.hh + i
                s1_b[2, q] = (part[2, pl.ds(q * 4, 4), c].astype(f32)
                              + rc_b[2, pl.ds(q * 4, 4)].astype(f32)).astype(bf16)
                return 0
            lax.fori_loop(0, 2, body, 0)
            for cp in self.xs:
                start(cp)

        def x_done(self):
            for cp in self.xs:
                cp.wait_recv()
            t = s1_b[2, self.planes, x].astype(f32)
            for j in range(3):
                t = t + rx_b[2, j, self.planes].astype(f32)
            s2g[self.q] = t.astype(bf16).reshape(4, R // 2, B)
            for cp in self.zs:
                start(cp)

        def z_done(self):
            for cp in self.zs:
                cp.wait_recv()
            t = s2g[self.q, z].astype(f32)
            for j in range(3):
                t = t + rzg[self.q, j].astype(f32)
            slab[1, h, 2 * self.hh + z // 2, x, c, z % 2] = t.astype(bf16)
            first = ((2 * self.hh + z // 2) * 8 + x * 2 + c) * R + (z % 2) * (R // 2)
            ri = first + lax.broadcasted_iota(jnp.int32, (R // 2, B), 0)
            ci = f * B + lax.broadcasted_iota(jnp.int32, (R // 2, B), 1)
            t = t + jnp.where(ri == ci, damping, 0.0)
            if self.q == 0:
                nsrc[1, 0] = total(t * t)
            else:
                nsrc[1, 0] += total(t * t)
            for cp in self.agz + (nz_cp[1] if self.q else []):
                start(cp)

        def agz_done(self):
            if self.q:
                gathered(1, self.agz + nz_cp[1], 0, 0, 7)
            else:
                for cp in self.agz:
                    cp.wait_recv()
            for cp in self.agx + (nx_cp[1] if self.q else []):
                start(cp)

        def agx_done(self):
            if self.q:
                gathered(1, self.agx + nx_cp[1], 1, 7, 3)
            else:
                for cp in self.agx:
                    cp.wait_recv()
            for cp in self.agc + (nc_cp[1] if self.q else []):
                start(cp)

        def agc_done(self):
            if self.q:
                gathered(1, self.agc + nc_cp[1], 2, 10, 1)
                for cp in ny_cp[1]:
                    start(cp)
            else:
                for cp in self.agc:
                    cp.wait_recv()

    ga, gb = Half(0), Half(1)

    def alpha_of(k):
        for cp in ny_cp[k - 1]:
            cp.wait_recv()
        t = nsrc[k - 1, 3]
        for i in range(3):
            t = t + nbuf[k - 1, 11 + i]
        return (1.0 / jnp.sqrt(t))[0:1, 0:1]

    def slab_rows(k, e, b):
        return slab[k - 1, e, b // 2, (b % 2) * 2:(b % 2) * 2 + 2].reshape(B, B)

    def both(k, block):
        cols = []
        for e in range(2):
            t = dot(block(0), slab_rows(k, e, 0))
            for b in range(1, 8):
                t = t + dot(block(b), slab_rows(k, e, b))
            cols.append(t)
        return jnp.concatenate(cols, axis=1)

    x_own = [None] * 6
    step_cp = [[copy(xg.at[i, y], xg.at[i, y], at(dy=j)) for j in (2, 1, 3)] for i in range(6)]

    def step_send(i, value):
        v = value.astype(bf16)
        xg[i, y, 0] = v[:, :B]
        xg[i, y, 1] = v[:, B:]
        x_own[i] = value
        for cp in step_cp[i]:
            start(cp)

    def step_mul(i, k):
        for cp in step_cp[i]:
            cp.wait_recv()
        return x_own[i] * damping + both(k, lambda b: xg[i, b % 4, b // 4])

    t_base = []
    for _ in range(2):
        t_base.append(count[0])
        count[0] += 4
    t_slot = (fd // 4) * 2 + pair
    t_pair = [copy(tpo.at[0, 0], tp.at[0, 0, c], at(dc=1)),
              copy(tpo.at[1], tp.at[1, :, c], at(dc=1))]

    def t_copy(i, e, m, slot):
        if i == 0:
            dev = {"dp": 4 * f + 2 * c + m, "fac": e * 4 + fd % 4}
        else:
            dev = {"dp": 4 * (e * 4 + y) + 2 * c + m, "fac": h * 4 + fd % 4}
        return pltpu.make_async_remote_copy(
            src_ref=tsrc.at[i, 0 if i == 0 else e, m], dst_ref=tdst.at[i, slot],
            send_sem=ssem.at[t_base[i] + e * 2 + m], recv_sem=rsem.at[t_base[i] + slot],
            device_id=dev, device_id_type=pl.DeviceIdType.MESH)

    def t_here(i, e, m):
        if i == 0:
            return own0 & (d == 4 * f + 2 * c + m) & (h == e)
        return own1 & (d == 4 * (e * 4 + y) + 2 * c + m)

    def t_core(i, value):
        for e in range(i + 1):
            lo = value[:, e * B:e * B + 128]
            hi = value[:, e * B + 128:(e + 1) * B]
            tp[i, e, c] = jnp.where(c == 0, lo, hi).astype(bf16)
            tpo[i, e] = jnp.where(c == 0, hi, lo).astype(bf16)
        start(t_pair[i])

    def t_send(i):
        t_pair[i].wait_recv()
        for e in range(i + 1):
            tsrc[i, e] = tp[i, e].astype(f32).reshape(128, 128).T.astype(bf16).reshape(2, R, 128)
        for e in range(2):
            for m in range(2):
                here = t_here(i, e, m)

                @pl.when(here)
                def _(e=e, m=m):
                    pltpu.make_async_copy(
                        tsrc.at[i, 0 if i == 0 else e, m], tdst.at[i, t_slot],
                        rsem.at[t_base[i] + t_slot]).start()

                @pl.when(jnp.logical_not(here))
                def _(e=e, m=m):
                    t_copy(i, e, m, t_slot).start()

    def t_recv(i):
        for k in range(4):
            t_copy(i, k // 2, k % 2, k).wait_recv()
        return jnp.concatenate([tdst[i, k].astype(f32) for k in range(4)], axis=1)

    lax.fori_loop(0, TOK // 32, norm, 0)
    gram(1, n_all, n_all)
    start(core_cp[1])
    g_cot.ring_fwd()
    core_done(1)
    for cp in w_x:
        cp.wait_recv()
    start(w_core)
    g_cot.middle(0)
    g_cot.middle(1)
    g_cot.own_half()
    g_cot.tail_fwd()
    x_done(1)
    g_cot.finish()
    w_core.wait_recv()

    acc[...] = jnp.zeros_like(acc)

    def og(b, _):
        w_blk = w_all[b // 2, pl.ds((b % 2) * 2, 2)].reshape(B, B)
        acc[...] += dot(cot_all[b], w_blk)
        return 0

    lax.fori_loop(0, 8, og, 0)
    for s in range(2):
        rows = pl.ds(s * ORBS, ORBS)
        og_s = (acc[rows, :] * keep_s[rows, :]).astype(bf16)
        for hd in range(2):
            v = dot_t(probs[s, hd], og_s[:, hd * 128:(hd + 1) * 128])
            v_all[f, rows, pl.ds(hd * 128, 128)] = v.astype(bf16)
    g_v.begin_z()
    g_v.begin_y()
    gram(0, n_all, v_all)
    start(core_cp[0])
    z_done(1)
    agz_start()
    core_done(0)
    g_v.ring_fwd()
    g_v.middle(0)
    x_done(0)
    g_v.own_half()
    ga.gram()
    g_v.middle(1)
    ga.core_done()
    agz_done()
    grad = z_done(0)
    t_core(0, grad)
    gx[f] = grad.astype(bf16)
    g_v.tail_fwd()
    t_send(0)
    ga.x_done()
    g_v.finish()
    gb.gram()
    ga.z_done()
    gb.core_done()
    x0 = t_recv(0)
    step_send(0, x0)
    agx_done()
    gb.x_done()
    agc_done()
    a_alpha = alpha_of(1)
    c1 = 4.0 * x0 - a_alpha * step_mul(0, 1)
    step_send(1, c1)
    gb.z_done()
    ga.agz_done()
    c2 = 6.0 * x0 - a_alpha * step_mul(1, 1)
    step_send(2, c2)
    gb.agz_done()
    for cp in gx_cp + [grad_part]:
        start(cp)
    ga.agx_done()
    c3 = 4.0 * x0 - a_alpha * step_mul(2, 1)
    t_core(1, c3)
    t_send(1)
    gb.agx_done()
    ga.agc_done()
    l0 = t_recv(1)
    step_send(3, l0)
    gb.agc_done()
    g_alpha = alpha_of(2)
    c1 = 4.0 * l0 - g_alpha * step_mul(3, 2)
    step_send(4, c1)
    for cp in gx_cp + [grad_part]:
        cp.wait_recv()
    grads = jnp.concatenate([grad2[0], grad2[1]], axis=1)
    q0 = both(2, lambda b: gx[b]) + damping * grads
    c2 = 6.0 * l0 - g_alpha * step_mul(4, 2)
    fin[0] = total(4.0 * grads * l0 - g_alpha * (q0 * c2))
    yc_offs = [(2, 0), (2, 1), (1, 0), (3, 0), (1, 1), (3, 1), (0, 1)]
    fa = [copy(fin.at[0], fin.at[1 + i], at(dy=a, dc=b)) for i, (a, b) in enumerate(yc_offs)]
    fx = [copy(fin.at[8], fin.at[9 + i], at(dz=a, dx=b)) for i, (a, b) in enumerate(dp_offs)]
    for cp in fa:
        start(cp)
    step_send(5, c2)
    for cp in fa:
        cp.wait_recv()
    t = fin[0]
    for i in range(7):
        t = t + fin[1 + i]
    fin[8] = t
    for cp in fx:
        start(cp)
    c3 = 4.0 * l0 - g_alpha * step_mul(5, 2)
    ab = a_alpha * g_alpha
    tt[0:R, :] = c3 * ab
    for cp in fx:
        cp.wait_recv()
    for i in range(15):
        t = t + fin[9 + i]
    inner = t[0:1, 0:1] * ab
    out[...] = tt[0:R, pl.ds(pl.multiple_of(h * B, B), B)] * (float(D) / jnp.sqrt(inner + epsilon))

    for cp in started:
        cp.wait_send()
    for i in range(2):
        for e in range(2):
            for m in range(2):
                @pl.when(jnp.logical_not(t_here(i, e, m)))
                def _(i=i, e=e, m=m):
                    t_copy(i, e, m, 0).wait_send()
    assert count[0] <= NSEM


def per_device(occupations, stream, norm_gain, probs, w_out, cotangent):
    vm = pl.BlockSpec(memory_space=pltpu.VMEM)
    hb = pl.BlockSpec(memory_space=pl.ANY)
    V = pltpu.VMEM
    return pl.pallas_call(
        kernel,
        out_shape=jax.ShapeDtypeStruct((R, B), f32),
        in_specs=[vm, hb, vm, hb, hb, hb],
        out_specs=vm,
        scratch_shapes=[
            V((8, TOK, B), bf16),
            V((8, TOK, B), bf16),
            V((8, TOK, B), bf16),
            V((8, TOK, B), bf16),
            V((4, 4, 2, R, B), bf16),
            V((2, 2, ORBS, ORBS), bf16),
            V((TOK, B), f32),
            V((TOK, 1), f32),
            V((3, 16, 2, R, B), bf16),
            V((16, 2, R, B), f32),
            V((4, 4, R, B), f32),
            V((4, R, B), f32),
            V((3, 16, R, B), bf16),
            V((3, 4, 4, R, B), bf16),
            V((3, 3, 4, R, B), bf16),
            V((3, 4, R, B), bf16),
            V((3, 3, R, B), bf16),
            V((2, 2, 4, 4, 2, 2, R // 2, B), bf16),
            V((2, 4, R // 2, B), bf16),
            V((2, 3, R // 2, B), bf16),
            V((2, R, B), f32),
            V((8, R, B), bf16),
            V((2, 2, 2, R, 128), bf16),
            V((2, 2, R, 128), bf16),
            V((2, 2, 2, R, 128), bf16),
            V((2, 4, R, 128), bf16),
            V((R, 2 * B), f32),
            V((6, 4, 2, R, B), bf16),
            V((2, 4, 8, 128), f32),
            V((2, 14, 8, 128), f32),
            V((24, 8, 128), f32),
            pltpu.SemaphoreType.DMA((4,)),
            pltpu.SemaphoreType.DMA((NSEM,)),
            pltpu.SemaphoreType.DMA((NSEM,)),
        ],
        compiler_params=pltpu.CompilerParams(
            collective_id=0, has_side_effects=True, vmem_limit_bytes=56 << 20),
    )(occupations, stream, norm_gain.reshape(1, D), probs, w_out.T, cotangent)


def solution(mesh):
    placed = (
        P("dp", None),
        P("dp", "fac"),
        P(),
        P("dp", "fac", None, None),
        P("fac", "dp"),
        P("dp", "fac"),
    )
    return jax.shard_map(
        per_device, mesh=mesh, in_specs=placed, out_specs=P("dp", "fac"), check_vma=False
    )
```
